32 devices in a mesh: fsdp: 32 (over z, y, x, core).
Axes of the slice: x: 2, y: 2, z: 4, core: 2. Of those that a mesh axis runs over, the one named last changes fastest.
Arguments:
- block_input: bfloat16 [32, 196, 512], P('fsdp'), may hold values from -6 to 6
- out_cotangent: bfloat16 [32, 196, 512], P('fsdp'), may hold values from -6 to 6
- norm1_gain: bfloat16 [512], P('fsdp'), may hold values from 0.099609375 to 1.8984375
- norm1_bias: bfloat16 [512], P('fsdp'), may hold values from -3 to 3
- qkv_weight: bfloat16 [512, 1536], P('fsdp'), may hold values from -0.25 to 0.25
- qv_bias: bfloat16 [1024], P('fsdp'), may hold values from -3 to 3
- proj_weight: bfloat16 [512, 512], P('fsdp'), may hold values from -1 to 1
- proj_bias: bfloat16 [512], P('fsdp'), may hold values from -3 to 3
- norm2_gain: bfloat16 [512], P('fsdp'), may hold values from 0.099609375 to 1.8984375
- norm2_bias: bfloat16 [512], P('fsdp'), may hold values from -3 to 3
- fc1_weight: bfloat16 [512, 2048], P('fsdp'), may hold values from -0.25 to 0.25
- fc1_bias: bfloat16 [2048], P('fsdp'), may hold values from -3 to 3
- fc2_weight: bfloat16 [2048, 512], P(None, 'fsdp'), may hold values from -0.125 to 0.125
- fc2_bias: bfloat16 [512], P('fsdp'), may hold values from -3 to 3
- bias_table: bfloat16 [169, 16], replicated, may hold values from -4 to 296
- window_mask: int32 [4, 49, 49], replicated, may hold values from 0 to 1, as said below
- rel_index: int32 [49, 49], replicated, may hold values from 0 to 168
- partition: int32 [196], replicated, may hold values from 0 to 195, each once
Outputs:
- block_output: bfloat16 [32, 196, 512], P('fsdp')
- input_grad: float32 [32, 196, 512], P('fsdp')
- norm1_gain_grad: float32 [512], P('fsdp')
- norm1_bias_grad: float32 [512], P('fsdp')
- qkv_weight_grad: float32 [512, 1536], P('fsdp')
- qv_bias_grad: float32 [1024], P('fsdp')
- proj_weight_grad: float32 [512, 512], P('fsdp')
- proj_bias_grad: float32 [512], P('fsdp')
- norm2_gain_grad: float32 [512], P('fsdp')
- norm2_bias_grad: float32 [512], P('fsdp')
- fc1_weight_grad: float32 [512, 2048], P('fsdp')
- fc1_bias_grad: float32 [2048], P('fsdp')
- fc2_weight_grad: float32 [2048, 512], P(None, 'fsdp')
- fc2_bias_grad: float32 [512], P('fsdp')
- bias_table_grad: float32 [169, 16], replicated
The draws below stay inside these ranges and needn't reach their ends.
Inputs may be any that keep to these rules, and one draw needn't show every extreme that they name: window_mask[w, i, j] is 1 exactly where positions i and j of window w carry the same region label; it is symmetric and 1 on the diagonal. `partition`: a permutation of 0 to 195.
All inputs are finite; a program needn't handle non-finite values.
Results may differ from the reference program's by a relative error of at most 0.011.
Values may be sent and summed in bfloat16 or wider, within the bound.
A program may use at most 128 MiB of HBM per device.

```python
import math
import jax
import jax.numpy as jnp
from jax import lax

D = 512
HEADS = 16
FF = 2048
HEAD_DIM = 32
WINDOW = 49
REL = 169
WIN_IMG = 4
TOK_IMG = 196
IMAGES = 32


def draw_window_mask(key, part):
    labels = jax.random.randint(key, (WIN_IMG, WINDOW), 0, 4)
    return (labels[:, :, None] == labels[:, None, :]).astype(jnp.int32)


def draw_bias_table(key, part):
    key_base = jax.random.fold_in(key, 11)
    table = jnp.clip(jax.random.normal(key_base, (REL, HEADS), jnp.float32), -4.0, 4.0)
    return table.astype(jnp.bfloat16)


def place_ends(drawn, stream_key, least, high):
    spot = [jax.random.randint(jax.random.fold_in(stream_key, axis), (), 0, length) for axis, length in enumerate(drawn.shape)]
    main_axis = drawn.shape.index(max(drawn.shape))
    beside = spot[:main_axis] + [(spot[main_axis] + 1) % drawn.shape[main_axis]] + spot[main_axis + 1:]
    return drawn.at[tuple(spot)].set(least).at[tuple(beside)].set(high)


def raised(values, key, source, target, shards_of, factor):
    owner, partner = [(jnp.arange(values.shape[dim]) // (values.shape[dim] // shards_of)).reshape([-1 if axis == dim else 1 for axis in range(values.ndim)]) for dim in (source, target)]
    chosen = jax.random.permutation(key, shards_of)[partner]
    strong = (owner == chosen) | (owner == (partner + shards_of // 2) % shards_of)
    return jnp.where(strong, factor * values, values)


def steps_of(key, extent, cuts, low, top_value):
    factor_of, own = 1.0, jax.random.fold_in(key, 6)
    for dim, parts in cuts:
        heights = jnp.exp(jax.random.uniform(jax.random.fold_in(own, dim), (parts,), jnp.float32, low / len(cuts), top_value / len(cuts)))
        factor_of = factor_of * jnp.repeat(heights, extent[dim] // parts).reshape([-1 if axis == dim else 1 for axis in range(len(extent))])
    return factor_of


def centred(own_key, shape, deviation, reach, shards=(), held_as=jnp.bfloat16):
    drawn = jax.random.normal(own_key, shape, jnp.float32) * deviation
    if len(shards) > 0:
        drawn = steps_of(own_key, shape, shards, -0.22, 0.18) * drawn
    return jnp.clip(drawn, min=-reach, max=reach).astype(held_as)


def heavy_noise(stream_key, dims, deviation, limit, cuts, heavy, held_as=jnp.bfloat16):
    drawn = deviation * jax.random.normal(stream_key, dims, jnp.float32)
    if cuts:
        drawn = drawn * steps_of(stream_key, dims, cuts, -0.22, 0.18)
    return jnp.clip(raised(drawn, jax.random.fold_in(stream_key, 3), *heavy), -limit, limit).astype(held_as)


def setup_inputs(seed: int = 0) -> dict:
    splits = jax.random.split(jax.random.key(seed), 19)
    return {
        "block_input": centred(splits[0], (IMAGES, TOK_IMG, D), 1.0, 6.0, ((0, 32),)),
        "out_cotangent": heavy_noise(splits[1], (IMAGES, TOK_IMG, D), 1.0, 6.0, ((0, 32),), (0, 2, 32, 2.75)),
        "norm1_gain": jnp.clip(1.0 + 0.18 * jax.random.normal(splits[2], (D,), jnp.float32), 0.099609375, 1.8984375).astype(jnp.bfloat16),
        "norm1_bias": centred(splits[3], (D,), 0.5, 3.0, ((0, 32),)),
        "qkv_weight": centred(splits[4], (D, 3 * D), D ** -0.5, 0.25, ((0, 32),)),
        "qv_bias": centred(splits[5], (2 * D,), 0.5, 3.0, ((0, 32),)),
        "proj_weight": centred(splits[6], (D, D), (D // 12) ** -0.5, 1.0, ((0, 32),)),
        "proj_bias": centred(splits[7], (D,), 0.5, 3.0, ((0, 32),)),
        "norm2_gain": jnp.clip(1.0 + 0.18 * jax.random.normal(splits[8], (D,), jnp.float32), 0.099609375, 1.8984375).astype(jnp.bfloat16),
        "norm2_bias": centred(splits[9], (D,), 0.5, 3.0, ((0, 32),)),
        "fc1_weight": centred(splits[10], (D, FF), D ** -0.5, 0.25, ((0, 32),)),
        "fc1_bias": centred(splits[11], (FF,), 0.5, 3.0, ((0, 32),)),
        "fc2_weight": centred(splits[12], (FF, D), FF ** -0.5, 0.125, ((1, 32),)),
        "fc2_bias": centred(splits[13], (D,), 0.5, 3.0, ((0, 32),)),
        "bias_table": draw_bias_table(jax.random.fold_in(splits[18], 71), 0),
        "window_mask": draw_window_mask(jax.random.fold_in(splits[18], 71), 0),
        "rel_index": place_ends(jax.random.randint(splits[16], (WINDOW, WINDOW), 0, REL), jax.random.fold_in(splits[16], 1), 0, REL - 1).astype(jnp.int32),
        "partition": jax.random.permutation(splits[17], TOK_IMG).astype(jnp.int32),
    }


EPSILON = 1e-05
NEG_FILL = -1e+30
ROOT_HALF = 0.7071067811865476
DENSITY = 0.3989422804014327

def normalize(values, gain_vec, shift_vec):
    center = values - lax.optimization_barrier(jnp.mean(values, axis=-1, keepdims=True))
    inv_std = lax.rsqrt(lax.optimization_barrier(jnp.mean(center * center, axis=-1, keepdims=True)) + EPSILON)
    unit_rows = center * inv_std
    return (unit_rows * gain_vec + shift_vec, unit_rows, inv_std)

def norm_backward(grad_out, unit_rows, inv_std, gain_vec):
    scaled = grad_out * gain_vec
    grad_in = inv_std * (scaled - lax.optimization_barrier(jnp.mean(scaled, axis=-1, keepdims=True)) - unit_rows * lax.optimization_barrier(jnp.mean(scaled * unit_rows, axis=-1, keepdims=True)))
    return (grad_in, lax.optimization_barrier(jnp.sum(grad_out * unit_rows, axis=0)), lax.optimization_barrier(jnp.sum(grad_out, axis=0)))

def gelu_parts(pre_act):
    normal_cdf = 0.5 * (1.0 + jax.scipy.special.erf(pre_act * ROOT_HALF))
    normal_pdf = jnp.exp(-0.5 * pre_act * pre_act) * DENSITY
    return (pre_act * normal_cdf, normal_cdf + pre_act * normal_pdf)

def to_windows(token_rows, partition):
    picked = jnp.take(token_rows, partition, axis=1)
    return picked.reshape(token_rows.shape[0], WIN_IMG, WINDOW, token_rows.shape[-1])

def from_windows(window_rows, inverse):
    flat_rows = window_rows.reshape(window_rows.shape[0], TOK_IMG, window_rows.shape[-1])
    return jnp.take(flat_rows, inverse, axis=1)

def reference(block_input, out_cotangent, norm1_gain, norm1_bias, qkv_weight, qv_bias, proj_weight, proj_bias, norm2_gain, norm2_bias, fc1_weight, fc1_bias, fc2_weight, fc2_bias, bias_table, window_mask, rel_index, partition):
    score_scale = HEAD_DIM ** (-0.5)
    inverse = jnp.argsort(partition).astype(jnp.int32)
    table_bias = jnp.transpose(bias_table.astype(jnp.float32)[rel_index], (2, 0, 1))
    allowed = (window_mask == 1)[None, :, None, :, :]
    gain_one = norm1_gain.astype(jnp.float32)
    shift_one = norm1_bias.astype(jnp.float32)
    gain_two = norm2_gain.astype(jnp.float32)
    shift_two = norm2_bias.astype(jnp.float32)
    qkv_shift = jnp.concatenate([qv_bias[:D].astype(jnp.float32), jnp.zeros((D,), jnp.float32), qv_bias[D:].astype(jnp.float32)])
    block_images = math.gcd(IMAGES, 16)
    row_count = block_images * TOK_IMG

    def scores_of(queries, key_rows):
        raw = jnp.einsum('bwihe,bwjhe->bwhij', queries.astype(jnp.float32), key_rows.astype(jnp.float32)) * score_scale + table_bias
        return jnp.where(allowed, raw, NEG_FILL)

    def process(totals, pieces):
        images, cotangent = pieces
        inputs_f = images.astype(jnp.float32).reshape(row_count, D)
        normed_one, unit_one, inv_one = normalize(inputs_f, gain_one, shift_one)
        normed_one = normed_one.astype(jnp.bfloat16)
        qkv_rows = (jnp.dot(normed_one, qkv_weight, preferred_element_type=jnp.float32) + qkv_shift).astype(jnp.bfloat16)
        qkv_win = to_windows(qkv_rows.reshape(block_images, TOK_IMG, 3 * D), partition).reshape(block_images, WIN_IMG, WINDOW, 3, HEADS, HEAD_DIM)
        queries = qkv_win[:, :, :, 0]
        key_rows = qkv_win[:, :, :, 1]
        value_rows = qkv_win[:, :, :, 2]
        scores = scores_of(queries, key_rows)
        row_top = lax.optimization_barrier(jnp.max(scores, axis=-1, keepdims=True))
        log_total = row_top + jnp.log(lax.optimization_barrier(jnp.sum(jnp.exp(scores - row_top), axis=-1, keepdims=True)))
        soft_full = jnp.exp(scores - log_total)
        soft_probs = soft_full.astype(jnp.bfloat16)
        mixed = jnp.einsum('bwhij,bwjhe->bwihe', soft_probs.astype(jnp.float32), value_rows.astype(jnp.float32))
        attended = from_windows(mixed.reshape(block_images, WIN_IMG, WINDOW, D), inverse).astype(jnp.bfloat16).reshape(row_count, D)
        resid = inputs_f + jnp.dot(attended, proj_weight, preferred_element_type=jnp.float32) + proj_bias.astype(jnp.float32)
        normed_two, unit_two, inv_two = normalize(resid, gain_two, shift_two)
        normed_two = normed_two.astype(jnp.bfloat16)
        pre_act = jnp.dot(normed_two, fc1_weight, preferred_element_type=jnp.float32) + fc1_bias.astype(jnp.float32)
        activ, gelu_slope = gelu_parts(pre_act)
        activ = activ.astype(jnp.bfloat16)
        output = (resid + jnp.dot(activ, fc2_weight, preferred_element_type=jnp.float32) + fc2_bias.astype(jnp.float32)).astype(jnp.bfloat16)
        cot_rows = cotangent.reshape(row_count, D)
        cot_f = cot_rows.astype(jnp.float32)
        fc2_grad = jnp.dot(activ.T, cot_rows, preferred_element_type=jnp.float32)
        fc2_bias_grad = lax.optimization_barrier(jnp.sum(cot_f, axis=0))
        grad_pre = jnp.dot(cot_rows, fc2_weight.T, preferred_element_type=jnp.float32) * gelu_slope
        grad_pre_b = grad_pre.astype(jnp.bfloat16)
        fc1_grad = jnp.dot(normed_two.T, grad_pre_b, preferred_element_type=jnp.float32)
        fc1_bias_grad = lax.optimization_barrier(jnp.sum(grad_pre, axis=0))
        grad_normed = jnp.dot(grad_pre_b, fc1_weight.T, preferred_element_type=jnp.float32)
        grad_mid, gain_two_grad, shift_two_grad = norm_backward(grad_normed, unit_two, inv_two, gain_two)
        grad_resid = cot_f + grad_mid
        grad_resid_b = grad_resid.astype(jnp.bfloat16)
        proj_grad = jnp.dot(attended.T, grad_resid_b, preferred_element_type=jnp.float32)
        proj_bias_grad = lax.optimization_barrier(jnp.sum(grad_resid, axis=0))
        grad_att = jnp.dot(grad_resid_b, proj_weight.T, preferred_element_type=jnp.float32).astype(jnp.bfloat16)
        grad_mixed = to_windows(grad_att.reshape(block_images, TOK_IMG, D), partition).reshape(block_images, WIN_IMG, WINDOW, HEADS, HEAD_DIM)
        value_grad = jnp.einsum('bwhij,bwihe->bwjhe', soft_probs.astype(jnp.float32), grad_mixed.astype(jnp.float32))
        prob_grad = jnp.einsum('bwihe,bwjhe->bwhij', grad_mixed.astype(jnp.float32), value_rows.astype(jnp.float32))
        score_grad = soft_full * (prob_grad - lax.optimization_barrier(jnp.sum(soft_full * prob_grad, axis=-1, keepdims=True)))
        pair_grad = lax.optimization_barrier(jnp.sum(score_grad, axis=(0, 1)))
        score_grad_b = score_grad.astype(jnp.bfloat16)
        query_grad = jnp.einsum('bwhij,bwjhe->bwihe', score_grad_b.astype(jnp.float32), key_rows.astype(jnp.float32)) * score_scale
        key_grad = jnp.einsum('bwhij,bwihe->bwjhe', score_grad_b.astype(jnp.float32), queries.astype(jnp.float32)) * score_scale
        stacked = jnp.stack([query_grad, key_grad, value_grad], axis=3).reshape(block_images, WIN_IMG, WINDOW, 3 * D)
        qkv_grad = from_windows(stacked, inverse).reshape(row_count, 3 * D)
        qkv_grad_b = qkv_grad.astype(jnp.bfloat16)
        qkv_grad_w = jnp.dot(normed_one.T, qkv_grad_b, preferred_element_type=jnp.float32)
        column_sums = lax.optimization_barrier(jnp.sum(qkv_grad, axis=0))
        qv_grad = jnp.concatenate([column_sums[:D], column_sums[2 * D:]])
        grad_first = jnp.dot(qkv_grad_b, qkv_weight.T, preferred_element_type=jnp.float32)
        grad_low, gain_one_grad, shift_one_grad = norm_backward(grad_first, unit_one, inv_one, gain_one)
        input_grad = (grad_resid + grad_low).reshape(block_images, TOK_IMG, D)
        grads = (gain_one_grad, shift_one_grad, qkv_grad_w, qv_grad, proj_grad, proj_bias_grad, gain_two_grad, shift_two_grad, fc1_grad, fc1_bias_grad, fc2_grad, fc2_bias_grad, pair_grad)
        new_totals = jax.tree.map(jnp.add, totals, grads)
        return (new_totals, (output.reshape(block_images, TOK_IMG, D), input_grad))
    zero_totals = (jnp.zeros((D,), jnp.float32), jnp.zeros((D,), jnp.float32), jnp.zeros((D, 3 * D), jnp.float32), jnp.zeros((2 * D,), jnp.float32), jnp.zeros((D, D), jnp.float32), jnp.zeros((D,), jnp.float32), jnp.zeros((D,), jnp.float32), jnp.zeros((D,), jnp.float32), jnp.zeros((D, FF), jnp.float32), jnp.zeros((FF,), jnp.float32), jnp.zeros((FF, D), jnp.float32), jnp.zeros((D,), jnp.float32), jnp.zeros((HEADS, WINDOW, WINDOW), jnp.float32))
    steps_count = IMAGES // block_images
    totals, (outputs, input_grads) = lax.scan(process, zero_totals, (block_input.reshape(steps_count, block_images, TOK_IMG, D), out_cotangent.reshape(steps_count, block_images, TOK_IMG, D)))
    pair_total = totals[12]
    table_grad = jnp.zeros((REL, HEADS), jnp.float32).at[rel_index.reshape(-1)].add(jnp.transpose(pair_total, (1, 2, 0)).reshape(WINDOW * WINDOW, HEADS))
    return (outputs.reshape(IMAGES, TOK_IMG, D), input_grads.reshape(IMAGES, TOK_IMG, D), totals[0], totals[1], totals[2], totals[3], totals[4], totals[5], totals[6], totals[7], totals[8], totals[9], totals[10], totals[11], table_grad)
```

```python
import functools

import jax
import jax.numpy as jnp
from jax import lax
from jax.experimental import pallas as pl
from jax.experimental.pallas import tpu as pltpu
from jax.sharding import PartitionSpec as P

HEADS = 16
WINDOW = 49
WIN_IMG = 4
MICRO = 1


EPSILON = 1e-05
NEG_FILL = -1e30
ROOT_HALF = 0.7071067811865476
DENSITY = 0.3989422804014327


def normalize(values, gain_vec, shift_vec):
    center = values - jnp.mean(values, axis=-1, keepdims=True)
    inv_std = lax.rsqrt(jnp.mean(center * center, axis=-1, keepdims=True) + EPSILON)
    unit_rows = center * inv_std
    return (unit_rows * gain_vec + shift_vec, unit_rows, inv_std)


def norm_backward(grad_out, unit_rows, inv_std, gain_vec):
    scaled = grad_out * gain_vec
    grad_in = inv_std * (
        scaled
        - jnp.mean(scaled, axis=-1, keepdims=True)
        - unit_rows * jnp.mean(scaled * unit_rows, axis=-1, keepdims=True)
    )
    return (grad_in, jnp.sum(grad_out * unit_rows, axis=0), jnp.sum(grad_out, axis=0))


def gelu_parts(pre_act):
    normal_cdf = 0.5 * (1.0 + jax.scipy.special.erf(pre_act * ROOT_HALF))
    normal_pdf = jnp.exp(-0.5 * pre_act * pre_act) * DENSITY
    return (pre_act * normal_cdf, normal_cdf + pre_act * normal_pdf)


def to_windows(token_rows, partition):
    picked = jnp.take(token_rows, partition, axis=1)
    return picked.reshape(token_rows.shape[0], WIN_IMG, WINDOW, token_rows.shape[-1])


def from_windows(window_rows, inverse):
    flat_rows = window_rows.reshape(window_rows.shape[0], inverse.shape[0], window_rows.shape[-1])
    return jnp.take(flat_rows, inverse, axis=1)


def window_scores(queries, key_rows, lookups, score_scale):
    table_bias, allowed, partition, inverse = lookups
    raw = (
        jnp.einsum("bwihe,bwjhe->bwhij", queries, key_rows, preferred_element_type=jnp.float32)
        * score_scale
        + table_bias
    )
    return jnp.where(allowed, raw, NEG_FILL)


MESH = pl.DeviceIdType.MESH


def bit_orders(bit_count):
    rest = list(range(1, bit_count))
    return ([0] + rest, [0] + rest[1:] + rest[:1])


def part_order(part, bit_count):
    return bit_orders(bit_count)[part % 2]


def place(bit_count):
    me = lax.axis_index("fsdp")
    mine = [lax.rem(lax.div(me, 1 << b), 2) for b in range(bit_count)]
    partner = [me + (1 - 2 * mine[b]) * (1 << b) for b in range(bit_count)]
    return (mine, partner)


def greet(partner):
    barrier = pltpu.get_barrier_semaphore()
    for other in partner:
        pl.semaphore_signal(barrier, inc=1, device_id=(other,), device_id_type=MESH)
    pl.semaphore_wait(barrier, len(partner))


def gather_kernel(bit_count, part_count, *refs):
    ins, outs = refs[:part_count], refs[part_count : 2 * part_count]
    send_sem, recv_sem, local_sem = refs[2 * part_count :]
    mine, partner = place(bit_count)
    locals_ = []
    whole_index = tuple(mine[b] for b in reversed(range(bit_count)))
    for p in range(part_count):
        copy = pltpu.make_async_copy(ins[p], outs[p].at[whole_index], local_sem.at[p])
        copy.start()
        locals_.append(copy)
    greet(partner)
    pending = [None] * part_count
    sent = []
    done = [[] for _ in range(part_count)]
    for step in range(bit_count):
        for p in range(part_count):
            bit = part_order(p, bit_count)[bit_count - 1 - step]
            if step == 1:
                locals_[p].wait()
            if pending[p] is not None:
                pending[p].wait_recv()
            index = tuple(
                slice(None) if b in done[p] else mine[b] for b in reversed(range(bit_count))
            )
            view = outs[p].at[index]
            copy = pltpu.make_async_remote_copy(
                src_ref=ins[p] if step == 0 else view,
                dst_ref=view,
                send_sem=send_sem.at[p, step],
                recv_sem=recv_sem.at[p, step],
                device_id=(partner[bit],),
                device_id_type=MESH,
            )
            copy.start()
            pending[p] = copy
            sent.append(copy)
            done[p].append(bit)
    for p in range(part_count):
        pending[p].wait_recv()
    for copy in sent:
        copy.wait_send()


def gather_parts(parts, count):
    bit_count = count.bit_length() - 1
    part_count = len(parts)
    spec = pl.BlockSpec(memory_space=pltpu.VMEM)
    outs = pl.pallas_call(
        functools.partial(gather_kernel, bit_count, part_count),
        out_shape=[
            jax.ShapeDtypeStruct((2,) * bit_count + part.shape, part.dtype) for part in parts
        ],
        in_specs=[spec] * part_count,
        out_specs=[spec] * part_count,
        scratch_shapes=[
            pltpu.SemaphoreType.DMA((part_count, bit_count)),
            pltpu.SemaphoreType.DMA((part_count, bit_count)),
            pltpu.SemaphoreType.DMA((part_count,)),
        ],
        compiler_params=pltpu.CompilerParams(collective_id=0, has_side_effects=True),
        name="gather_parts",
    )(*parts)
    return [out.reshape((count,) + part.shape) for out, part in zip(outs, parts)]


def scatter_kernel(bit_count, part_count, *refs):
    count = 1 << bit_count
    ins, table_in = refs[:part_count], refs[part_count]
    outs, table_out = refs[part_count + 1 : 2 * part_count + 1], refs[2 * part_count + 1]
    rest = list(refs[2 * part_count + 2 :])
    send_sem, recv_sem, table_send, table_recv = rest[:4]
    table_got, table_sum = rest[4:6]
    got = rest[6 : 6 + part_count * bit_count]
    held = rest[6 + part_count * bit_count :]
    mine, partner = place(bit_count)
    greet(partner)
    sent = []

    def table_start(step):
        copy = pltpu.make_async_remote_copy(
            src_ref=table_in if step == 0 else table_sum.at[step - 1],
            dst_ref=table_got.at[step],
            send_sem=table_send.at[step],
            recv_sem=table_recv.at[step],
            device_id=(partner[step],),
            device_id_type=MESH,
        )
        copy.start()
        sent.append(copy)
        return copy

    def start(p, step):
        bit = part_order(p, bit_count)[step]
        source = ins[p] if step == 0 else held[p * (bit_count - 1) + step - 1]
        copy = pltpu.make_async_remote_copy(
            src_ref=source.at[:, 1 - mine[bit]],
            dst_ref=got[p * bit_count + step],
            send_sem=send_sem.at[p, step],
            recv_sem=recv_sem.at[p, step],
            device_id=(partner[bit],),
            device_id_type=MESH,
        )
        copy.start()
        sent.append(copy)
        return copy

    def add(p, step):
        bit = part_order(p, bit_count)[step]
        source = ins[p] if step == 0 else held[p * (bit_count - 1) + step - 1]
        arrived = got[p * bit_count + step]
        high, low = arrived.shape[0], arrived.shape[1]

        def total(k):
            i, j = k // low, k % low
            return source[i, mine[bit], j].astype(jnp.float32) + arrived[i, j].astype(jnp.float32)

        if step == bit_count - 1:
            outs[p][...] = total(0)
            return
        target = held[p * (bit_count - 1) + step]
        low_next = target.shape[2]

        def body(k, carry):
            target[k // (2 * low_next), (k // low_next) % 2, k % low_next] = total(k).astype(
                target.dtype
            )
            return carry

        lax.fori_loop(0, high * low, body, 0)

    pending = [start(p, 0) for p in range(part_count)]
    table_pending = table_start(0)
    for step in range(bit_count):
        for p in range(part_count):
            pending[p].wait_recv()
            add(p, step)
            if step + 1 < bit_count:
                pending[p] = start(p, step + 1)
        table_pending.wait_recv()
        total_table = (table_in[...] if step == 0 else table_sum[step - 1]) + table_got[step]
        if step + 1 < bit_count:
            table_sum[step] = total_table
            table_pending = table_start(step + 1)
        else:
            table_out[...] = total_table
    for copy in sent:
        copy.wait_send()


def remaining_shape(order, step):
    left = sorted(order[step:])
    place_of = left.index(order[step])
    return (1 << (len(left) - 1 - place_of), 2, 1 << place_of)


def scatter_parts(parts, table, count):
    bit_count = count.bit_length() - 1
    part_count = len(parts)
    spec = pl.BlockSpec(memory_space=pltpu.VMEM)
    got, held, shaped = [], [], []
    for p, part in enumerate(parts):
        order = part_order(p, bit_count)
        block = part.shape[1:]
        for step in range(bit_count):
            high, two, low = remaining_shape(order, step)
            got.append(pltpu.VMEM((high, low) + block, part.dtype))
            if step == 0:
                shaped.append(part.reshape((high, two, low) + block))
            else:
                held.append(pltpu.VMEM((high, two, low) + block, part.dtype))
    outs = pl.pallas_call(
        functools.partial(scatter_kernel, bit_count, part_count),
        out_shape=[jax.ShapeDtypeStruct(part.shape[1:], jnp.float32) for part in parts]
        + [jax.ShapeDtypeStruct(table.shape, jnp.float32)],
        in_specs=[spec] * (part_count + 1),
        out_specs=[spec] * (part_count + 1),
        scratch_shapes=[
            pltpu.SemaphoreType.DMA((part_count, bit_count)),
            pltpu.SemaphoreType.DMA((part_count, bit_count)),
            pltpu.SemaphoreType.DMA((bit_count,)),
            pltpu.SemaphoreType.DMA((bit_count,)),
            pltpu.VMEM((bit_count,) + table.shape, jnp.float32),
            pltpu.VMEM((bit_count,) + table.shape, jnp.float32),
        ]
        + got
        + held,
        compiler_params=pltpu.CompilerParams(collective_id=1, has_side_effects=True),
        name="scatter_parts",
    )(*shaped, table)
    return (outs[:part_count], outs[part_count])


LANES = 128
ROWS = 16


def fold(block):
    r, c = block.shape[-2:]
    rows = max(r, ROWS)
    return block.reshape(block.shape[:-2] + (rows, r * c // rows))


def unfold(blocks, r, c):
    return blocks[..., : r * c // blocks.shape[-2]].reshape(blocks.shape[:-2] + (r, c))


def with_vectors(block, flat):
    rows, width = block.shape[-2:]
    extra = -(-flat.shape[-1] // rows)
    total = -(-(width + extra) // LANES) * LANES - width
    padded = jnp.pad(flat, [(0, 0)] * (flat.ndim - 1) + [(0, rows * total - flat.shape[-1])])
    return jnp.concatenate([block, padded.reshape(flat.shape[:-1] + (rows, total))], axis=-1)


def fetch_all(shards):
    count = lax.axis_size("fsdp")
    vectors = [shards[k] for k in (0, 1, 3, 5, 6, 7, 9, 11)]
    lengths = [v.shape[0] for v in vectors]
    qkv, proj, fc1, fc2_t = shards[2], shards[4], shards[8], shards[10].T
    folded_proj = fold(proj)
    parts = [
        fold(fc1),
        fold(fc2_t),
        fold(qkv),
        with_vectors(folded_proj, jnp.concatenate(vectors)),
    ]
    fc1_all, fc2_all, qkv_all, proj_all = gather_parts(parts, count)

    def whole(blocks, shard):
        r, c = shard.shape
        return unfold(blocks, r, c).reshape(count * r, c)

    flat = proj_all[:, :, folded_proj.shape[1] :].reshape(count, -1)
    start, gathered = 0, []
    for length in lengths:
        gathered.append(flat[:, start : start + length].reshape(-1))
        start += length
    return (
        gathered[0],
        gathered[1],
        whole(qkv_all, qkv),
        gathered[2],
        whole(proj_all, proj),
        gathered[3],
        gathered[4],
        gathered[5],
        whole(fc1_all, fc1),
        gathered[6],
        whole(fc2_all, fc2_t),
        gathered[7],
    )


def scatter_whole(grads, table_local):
    count = lax.axis_size("fsdp")

    def blocks(grad):
        return fold(grad.astype(jnp.bfloat16).reshape(count, grad.shape[0] // count, grad.shape[1]))

    vectors = [
        grads[k].astype(jnp.bfloat16).reshape(count, -1) for k in (0, 1, 3, 5, 6, 7, 9, 11)
    ]
    folded_proj = blocks(grads[4])
    parts = [
        blocks(grads[10]),
        blocks(grads[8]),
        blocks(grads[2]),
        with_vectors(folded_proj, jnp.concatenate(vectors, axis=1)),
    ]
    entries = table_local.size
    table_rows = -(-entries // (8 * LANES)) * 8
    table_pad = jnp.pad(table_local.reshape(-1), (0, table_rows * LANES - entries)).reshape(
        table_rows, LANES
    )
    (fc2_b, fc1_b, qkv_b, proj_b), table_sum = scatter_parts(parts, table_pad, count)

    def own(block, grad):
        return unfold(block, grad.shape[0] // count, grad.shape[1])

    flat = proj_b[:, folded_proj.shape[2] :].reshape(-1)
    start, pieces = 0, []
    for vector in vectors:
        pieces.append(flat[start : start + vector.shape[1]])
        start += vector.shape[1]
    table_grad = table_sum.reshape(-1)[:entries].reshape(table_local.shape)
    return (
        (
            pieces[0],
            pieces[1],
            own(qkv_b, grads[2]),
            pieces[2],
            own(proj_b, grads[4]),
            pieces[3],
            pieces[4],
            pieces[5],
            own(fc1_b, grads[8]),
            pieces[6],
            own(fc2_b, grads[10]).T,
            pieces[7],
        ),
        table_grad,
    )


def forward_pass(images, params, lookups):
    (
        gain_one,
        shift_one,
        qkv_weight,
        qv_bias,
        proj_weight,
        proj_bias,
        gain_two,
        shift_two,
        fc1_weight,
        fc1_bias,
        fc2_weight,
        fc2_bias,
    ) = params
    table_bias, allowed, partition, inverse = lookups
    image_count, tok_count, model_width = images.shape
    row_count = image_count * tok_count
    head_width = model_width // HEADS
    score_scale = head_width ** (-0.5)
    inputs_f = images.astype(jnp.float32).reshape(row_count, model_width)
    normed_one, unit_one, inv_one = normalize(
        inputs_f, gain_one.astype(jnp.float32), shift_one.astype(jnp.float32)
    )
    normed_one = normed_one.astype(jnp.bfloat16)
    qkv_shift = jnp.concatenate(
        [
            qv_bias[:model_width].astype(jnp.float32),
            jnp.zeros((model_width,), jnp.float32),
            qv_bias[model_width:].astype(jnp.float32),
        ]
    )
    qkv_rows = (
        jnp.dot(normed_one, qkv_weight, preferred_element_type=jnp.float32) + qkv_shift
    ).astype(jnp.bfloat16)
    qkv_win = to_windows(
        qkv_rows.reshape(image_count, tok_count, 3 * model_width), partition
    ).reshape(image_count, WIN_IMG, WINDOW, 3, HEADS, head_width)
    scores = window_scores(qkv_win[:, :, :, 0], qkv_win[:, :, :, 1], lookups, score_scale)
    row_top = jnp.max(scores, axis=-1, keepdims=True)
    log_total = row_top + jnp.log(jnp.sum(jnp.exp(scores - row_top), axis=-1, keepdims=True))
    soft_probs = jnp.exp(scores - log_total).astype(jnp.bfloat16)
    mixed = jnp.einsum(
        "bwhij,bwjhe->bwihe", soft_probs, qkv_win[:, :, :, 2], preferred_element_type=jnp.float32
    )
    attended = (
        from_windows(mixed.reshape(image_count, WIN_IMG, WINDOW, model_width), inverse)
        .astype(jnp.bfloat16)
        .reshape(row_count, model_width)
    )
    resid = (
        inputs_f
        + jnp.dot(attended, proj_weight, preferred_element_type=jnp.float32)
        + proj_bias.astype(jnp.float32)
    )
    normed_two, unit_two, inv_two = normalize(
        resid, gain_two.astype(jnp.float32), shift_two.astype(jnp.float32)
    )
    normed_two = normed_two.astype(jnp.bfloat16)
    pre_act = jnp.dot(normed_two, fc1_weight, preferred_element_type=jnp.float32) + fc1_bias.astype(
        jnp.float32
    )
    activ, gelu_slope = gelu_parts(pre_act)
    activ = activ.astype(jnp.bfloat16)
    output = (
        resid
        + jnp.dot(activ, fc2_weight.T, preferred_element_type=jnp.float32)
        + fc2_bias.astype(jnp.float32)
    ).astype(jnp.bfloat16)
    saved = (
        unit_one,
        inv_one,
        normed_one,
        qkv_win,
        log_total,
        attended,
        unit_two,
        inv_two,
        normed_two,
        gelu_slope,
        activ,
    )
    return (output.reshape(image_count, tok_count, model_width), saved)


def backward_pass(cotangent, saved, params, lookups):
    (
        gain_one,
        shift_one,
        qkv_weight,
        qv_bias,
        proj_weight,
        proj_bias,
        gain_two,
        shift_two,
        fc1_weight,
        fc1_bias,
        fc2_weight,
        fc2_bias,
    ) = params
    (
        unit_one,
        inv_one,
        normed_one,
        qkv_win,
        log_total,
        attended,
        unit_two,
        inv_two,
        normed_two,
        gelu_slope,
        activ,
    ) = saved
    table_bias, allowed, partition, inverse = lookups
    image_count, tok_count, model_width = cotangent.shape
    row_count = image_count * tok_count
    head_width = model_width // HEADS
    score_scale = head_width ** (-0.5)
    cot_rows = cotangent.reshape(row_count, model_width)
    cot_f = cot_rows.astype(jnp.float32)
    fc2_grad = jnp.dot(cot_rows.T, activ, preferred_element_type=jnp.float32)
    fc2_bias_grad = jnp.sum(cot_f, axis=0)
    grad_pre = jnp.dot(cot_rows, fc2_weight, preferred_element_type=jnp.float32) * gelu_slope
    grad_pre_b = grad_pre.astype(jnp.bfloat16)
    fc1_grad = jnp.dot(normed_two.T, grad_pre_b, preferred_element_type=jnp.float32)
    fc1_bias_grad = jnp.sum(grad_pre, axis=0)
    grad_normed = jnp.dot(grad_pre_b, fc1_weight.T, preferred_element_type=jnp.float32)
    grad_mid, gain_two_grad, shift_two_grad = norm_backward(
        grad_normed, unit_two, inv_two, gain_two.astype(jnp.float32)
    )
    grad_resid = cot_f + grad_mid
    grad_resid_b = grad_resid.astype(jnp.bfloat16)
    proj_grad = jnp.dot(attended.T, grad_resid_b, preferred_element_type=jnp.float32)
    proj_bias_grad = jnp.sum(grad_resid, axis=0)
    grad_att = jnp.dot(grad_resid_b, proj_weight.T, preferred_element_type=jnp.float32).astype(
        jnp.bfloat16
    )
    grad_mixed = to_windows(
        grad_att.reshape(image_count, tok_count, model_width), partition
    ).reshape(image_count, WIN_IMG, WINDOW, HEADS, head_width)
    queries = qkv_win[:, :, :, 0]
    key_rows = qkv_win[:, :, :, 1]
    value_rows = qkv_win[:, :, :, 2]
    scores = window_scores(queries, key_rows, lookups, score_scale)
    soft_full = jnp.exp(scores - log_total)
    soft_probs = soft_full.astype(jnp.bfloat16)
    value_grad = jnp.einsum(
        "bwhij,bwihe->bwjhe", soft_probs, grad_mixed, preferred_element_type=jnp.float32
    )
    prob_grad = jnp.einsum(
        "bwihe,bwjhe->bwhij", grad_mixed, value_rows, preferred_element_type=jnp.float32
    )
    score_grad = soft_full * (prob_grad - jnp.sum(soft_full * prob_grad, axis=-1, keepdims=True))
    pair_grad = jnp.sum(score_grad, axis=(0, 1))
    score_grad_b = score_grad.astype(jnp.bfloat16)
    query_grad = (
        jnp.einsum("bwhij,bwjhe->bwihe", score_grad_b, key_rows, preferred_element_type=jnp.float32)
        * score_scale
    )
    key_grad = (
        jnp.einsum("bwhij,bwihe->bwjhe", score_grad_b, queries, preferred_element_type=jnp.float32)
        * score_scale
    )
    stacked = jnp.stack([query_grad, key_grad, value_grad], axis=3).reshape(
        image_count, WIN_IMG, WINDOW, 3 * model_width
    )
    qkv_grad = from_windows(stacked, inverse).reshape(row_count, 3 * model_width)
    qkv_grad_b = qkv_grad.astype(jnp.bfloat16)
    qkv_grad_w = jnp.dot(normed_one.T, qkv_grad_b, preferred_element_type=jnp.float32)
    column_sums = jnp.sum(qkv_grad, axis=0)
    qv_grad = jnp.concatenate([column_sums[:model_width], column_sums[2 * model_width :]])
    grad_first = jnp.dot(qkv_grad_b, qkv_weight.T, preferred_element_type=jnp.float32)
    grad_low, gain_one_grad, shift_one_grad = norm_backward(
        grad_first, unit_one, inv_one, gain_one.astype(jnp.float32)
    )
    input_grad = (grad_resid + grad_low).reshape(image_count, tok_count, model_width)
    grads = (
        gain_one_grad,
        shift_one_grad,
        qkv_grad_w,
        qv_grad,
        proj_grad,
        proj_bias_grad,
        gain_two_grad,
        shift_two_grad,
        fc1_grad,
        fc1_bias_grad,
        fc2_grad,
        fc2_bias_grad,
    )
    return (input_grad, grads, pair_grad)


def per_device(
    block_input,
    out_cotangent,
    norm1_gain,
    norm1_bias,
    qkv_weight,
    qv_bias,
    proj_weight,
    proj_bias,
    norm2_gain,
    norm2_bias,
    fc1_weight,
    fc1_bias,
    fc2_weight,
    fc2_bias,
    bias_table,
    window_mask,
    rel_index,
    partition,
):
    shards = (
        norm1_gain,
        norm1_bias,
        qkv_weight,
        qv_bias,
        proj_weight,
        proj_bias,
        norm2_gain,
        norm2_bias,
        fc1_weight,
        fc1_bias,
        fc2_weight,
        fc2_bias,
    )
    pair_count = WINDOW * WINDOW
    table_rows = bias_table.shape[0]
    one_hot = (
        rel_index.reshape(pair_count, 1) == jnp.arange(table_rows, dtype=jnp.int32)[None, :]
    ).astype(jnp.float32)
    table_bias = jnp.transpose(
        jnp.dot(one_hot, bias_table.astype(jnp.float32), precision=lax.Precision.HIGHEST).reshape(
            WINDOW, WINDOW, HEADS
        ),
        (2, 0, 1),
    )
    allowed = (window_mask == 1)[None, :, None, :, :]
    tok_count = partition.shape[0]
    inverse = (
        jnp.zeros((tok_count,), jnp.int32).at[partition].set(jnp.arange(tok_count, dtype=jnp.int32))
    )
    lookups = (table_bias, allowed, partition, inverse)
    held_params = fetch_all(shards)
    micro_index = 0
    output, saved = forward_pass(block_input, held_params, lookups)
    kept = [saved]
    input_grads = [None] * MICRO
    pair_total = jnp.zeros((HEADS, WINDOW, WINDOW), jnp.float32)
    grad_totals = None
    for micro_index in reversed(range(MICRO)):
        input_grad, grads, pair_grad = backward_pass(
            out_cotangent, kept[micro_index], held_params, lookups
        )
        input_grads[micro_index] = input_grad
        pair_total = pair_grad
        grad_totals = grads
    table_local = jnp.dot(
        one_hot.T,
        jnp.transpose(pair_total, (1, 2, 0)).reshape(pair_count, HEADS),
        precision=lax.Precision.HIGHEST,
    )
    grad_totals, table_grad = scatter_whole(grad_totals, table_local)
    input_grad_all = input_grads[0]
    return (
        output,
        input_grad_all,
        grad_totals[0],
        grad_totals[1],
        grad_totals[2],
        grad_totals[3],
        grad_totals[4],
        grad_totals[5],
        grad_totals[6],
        grad_totals[7],
        grad_totals[8],
        grad_totals[9],
        grad_totals[10],
        grad_totals[11],
        table_grad,
    )


def solution(mesh):
    placed = (
        P("fsdp", None, None),
        P("fsdp", None, None),
        P("fsdp"),
        P("fsdp"),
        P("fsdp", None),
        P("fsdp"),
        P("fsdp", None),
        P("fsdp"),
        P("fsdp"),
        P("fsdp"),
        P("fsdp", None),
        P("fsdp"),
        P(None, "fsdp"),
        P("fsdp"),
        P(),
        P(),
        P(),
        P(),
    )
    return jax.shard_map(
        per_device,
        mesh=mesh,
        in_specs=placed,
        out_specs=(
            P("fsdp", None, None),
            P("fsdp", None, None),
            P("fsdp"),
            P("fsdp"),
            P("fsdp", None),
            P("fsdp"),
            P("fsdp", None),
            P("fsdp"),
            P("fsdp"),
            P("fsdp"),
            P("fsdp", None),
            P("fsdp"),
            P(None, "fsdp"),
            P("fsdp"),
            P(),
        ),
        check_vma=False,
    )
```

```python
import functools

import jax
import jax.numpy as jnp
from jax import lax
from jax.experimental import pallas as pl
from jax.experimental.pallas import tpu as pltpu
from jax.sharding import PartitionSpec as P

HEADS = 16
WINDOW = 49
WIN_IMG = 4
MICRO = 1


EPSILON = 1e-05
NEG_FILL = -1e30
ROOT_HALF = 0.7071067811865476
DENSITY = 0.3989422804014327


def normalize(values, gain_vec, shift_vec):
    center = values - jnp.mean(values, axis=-1, keepdims=True)
    inv_std = lax.rsqrt(jnp.mean(center * center, axis=-1, keepdims=True) + EPSILON)
    unit_rows = center * inv_std
    return (unit_rows * gain_vec + shift_vec, unit_rows, inv_std)


def norm_backward(grad_out, unit_rows, inv_std, gain_vec):
    scaled = grad_out * gain_vec
    grad_in = inv_std * (
        scaled
        - jnp.mean(scaled, axis=-1, keepdims=True)
        - unit_rows * jnp.mean(scaled * unit_rows, axis=-1, keepdims=True)
    )
    return (grad_in, jnp.sum(grad_out * unit_rows, axis=0), jnp.sum(grad_out, axis=0))


def gelu_parts(pre_act):
    normal_cdf = 0.5 * (1.0 + jax.scipy.special.erf(pre_act * ROOT_HALF))
    normal_pdf = jnp.exp(-0.5 * pre_act * pre_act) * DENSITY
    return (pre_act * normal_cdf, normal_cdf + pre_act * normal_pdf)


NT = (((1,), (1,)), ((), ()))
TN = (((0,), (0,)), ((), ()))


def mul(left, right, dims=(((1,), (0,)), ((), ()))):
    return lax.dot_general(left, right, dims, preferred_element_type=jnp.float32)


def pair_mask(mask_ref, spread, same_ref):
    return (mul(mask_ref[...], spread) > 0.5) & (same_ref[...] > 0)


def head_scores(query, key_block, bias, spread_t, spread, allowed, scale):
    wide = mul(mul(spread_t, bias).astype(jnp.bfloat16), spread)
    return jnp.where(allowed, mul(query, key_block, NT) * scale + wide, NEG_FILL)


def soft_rows(scores):
    row_top = jnp.max(scores, axis=-1, keepdims=True)
    log_total = row_top + jnp.log(jnp.sum(jnp.exp(scores - row_top), axis=-1, keepdims=True))
    return jnp.exp(scores - log_total)


def head_lanes(rows, lanes, width, h):
    lane = lax.broadcasted_iota(jnp.int32, (rows, lanes), 1)
    return (lane >= h * width) & (lane < (h + 1) * width)


def attend_kernel(
    width, qkv_ref, pick_ref, back_ref, bias_ref, mask_ref, same_ref, spread_ref, spread_t_ref,
    qkv_win_ref, out_ref
):
    rows, model = out_ref.shape
    spread, spread_t = spread_ref[...], spread_t_ref[...]
    allowed = pair_mask(mask_ref, spread, same_ref)
    qkv_win_ref[...] = mul(pick_ref[...], qkv_ref[...]).astype(jnp.bfloat16)
    heads = LANES // width
    for group in range(model // LANES):
        low = group * LANES
        query = qkv_win_ref[:, low : low + LANES]
        keys = qkv_win_ref[:, model + low : model + low + LANES]
        values = qkv_win_ref[:, 2 * model + low : 2 * model + low + LANES]
        total = jnp.zeros((rows, LANES), jnp.float32)
        for h in range(heads):
            lanes = head_lanes(rows, LANES, width, h)
            scores = head_scores(
                jnp.where(lanes, query, jnp.zeros_like(query)),
                keys,
                bias_ref[group * heads + h],
                spread_t,
                spread,
                allowed,
                width ** (-0.5),
            )
            probs = soft_rows(scores).astype(jnp.bfloat16)
            total = jnp.where(lanes, mul(probs, values), total)
        out_ref[:, low : low + LANES] = mul(back_ref[...], total.astype(jnp.bfloat16)).astype(
            jnp.bfloat16
        )


def attend_back_kernel(
    width, qkv_win_ref, grad_ref, pick_ref, back_ref, bias_ref, mask_ref, same_ref, spread_ref,
    spread_t_ref, out_ref, sums_ref, pair_ref
):
    rows, model = grad_ref.shape
    spread, spread_t = spread_ref[...], spread_t_ref[...]
    allowed = pair_mask(mask_ref, spread, same_ref)
    heads = LANES // width
    scale = width ** (-0.5)
    for group in range(model // LANES):
        low = group * LANES
        query = qkv_win_ref[:, low : low + LANES]
        keys = qkv_win_ref[:, model + low : model + low + LANES]
        values = qkv_win_ref[:, 2 * model + low : 2 * model + low + LANES]
        grad = mul(pick_ref[...], grad_ref[:, low : low + LANES]).astype(jnp.bfloat16)
        totals = [jnp.zeros((rows, LANES), jnp.float32) for _ in range(3)]
        for h in range(heads):
            lanes = head_lanes(rows, LANES, width, h)
            scores = head_scores(
                jnp.where(lanes, query, jnp.zeros_like(query)),
                keys,
                bias_ref[group * heads + h],
                spread_t,
                spread,
                allowed,
                scale,
            )
            soft = soft_rows(scores)
            prob_grad = mul(jnp.where(lanes, grad, jnp.zeros_like(grad)), values, NT)
            inner = jnp.sum(soft * prob_grad, axis=-1, keepdims=True)
            score_grad = soft * (prob_grad - inner)
            coarse = score_grad.astype(jnp.bfloat16)
            fine = (score_grad - coarse.astype(jnp.float32)).astype(jnp.bfloat16)
            pair = jnp.zeros(pair_ref.shape[1:], jnp.float32)
            for piece in (coarse, fine):
                pair += mul(mul(spread, piece).astype(jnp.bfloat16), spread_t)
            pair_ref[group * heads + h] = pair
            totals[0] = jnp.where(lanes, mul(coarse, keys) * scale, totals[0])
            totals[1] = jnp.where(lanes, mul(coarse, query, TN) * scale, totals[1])
            totals[2] = jnp.where(lanes, mul(soft.astype(jnp.bfloat16), grad, TN), totals[2])
        for k in range(3):
            at = k * model + low
            sums_ref[:, at : at + LANES] = jnp.sum(totals[k], axis=0, keepdims=True)
            out_ref[:, at : at + LANES] = mul(
                back_ref[...], totals[k].astype(jnp.bfloat16)
            ).astype(jnp.bfloat16)


def attention_tables(bias_heads, window_mask, partition):
    tokens = partition.shape[0]
    span = window_mask.shape[-1]
    token = jnp.arange(tokens, dtype=jnp.int32)
    pick = (partition[:, None] == token[None, :]).astype(jnp.bfloat16)
    back = (partition[None, :] == token[:, None]).astype(jnp.bfloat16)
    same = (token[:, None] // span == token[None, :] // span).astype(jnp.float32)
    spread = (token[None, :] % span == jnp.arange(span)[:, None]).astype(jnp.bfloat16)
    mask_rows = (window_mask == 1).astype(jnp.bfloat16).reshape(tokens, span)
    return (pick, back, bias_heads.astype(jnp.bfloat16), mask_rows, same, spread, spread.T)


def attend(qkv_rows, tables):
    rows, wide = qkv_rows.shape
    model = wide // 3
    spec = pl.BlockSpec(memory_space=pltpu.VMEM)
    return pl.pallas_call(
        functools.partial(attend_kernel, model // HEADS),
        out_shape=[
            jax.ShapeDtypeStruct((rows, wide), jnp.bfloat16),
            jax.ShapeDtypeStruct((rows, model), jnp.bfloat16),
        ],
        in_specs=[spec] * 8,
        out_specs=[spec] * 2,
        name="attend",
    )(qkv_rows, *tables)


def attend_back(qkv_win, grad_att, tables):
    rows, wide = qkv_win.shape
    model = wide // 3
    span = tables[3].shape[1]
    spec = pl.BlockSpec(memory_space=pltpu.VMEM)
    return pl.pallas_call(
        functools.partial(attend_back_kernel, model // HEADS),
        out_shape=[
            jax.ShapeDtypeStruct((rows, wide), jnp.bfloat16),
            jax.ShapeDtypeStruct((1, wide), jnp.float32),
            jax.ShapeDtypeStruct((HEADS, span, span), jnp.float32),
        ],
        in_specs=[spec] * 9,
        out_specs=[spec] * 3,
        name="attend_back",
    )(qkv_win, grad_att, *tables)


LANES = 128
MESH = pl.DeviceIdType.MESH


def bit_orders(bit_count):
    rest = list(range(1, bit_count))
    return ([0] + rest, [0] + rest[1:] + rest[:1])


def part_order(part, bit_count):
    return bit_orders(bit_count)[part % 2]


def place(bit_count):
    me = lax.axis_index("fsdp")
    mine = [lax.rem(lax.div(me, 1 << b), 2) for b in range(bit_count)]
    partner = [me + (1 - 2 * mine[b]) * (1 << b) for b in range(bit_count)]
    return (mine, partner)


def greet(partner):
    barrier = pltpu.get_barrier_semaphore()
    for other in partner:
        pl.semaphore_signal(barrier, inc=1, device_id=(other,), device_id_type=MESH)
    pl.semaphore_wait(barrier, len(partner))


def gather_kernel(bit_count, part_count, *refs):
    ins, outs = refs[:part_count], refs[part_count : 2 * part_count]
    send_sem, recv_sem, local_sem = refs[2 * part_count :]
    mine, partner = place(bit_count)
    locals_ = []
    whole_index = tuple(mine[b] for b in reversed(range(bit_count)))
    for p in range(part_count):
        copy = pltpu.make_async_copy(ins[p], outs[p].at[whole_index], local_sem.at[p])
        copy.start()
        locals_.append(copy)
    greet(partner)
    pending = [None] * part_count
    sent = []
    done = [[] for _ in range(part_count)]
    for step in range(bit_count):
        for p in range(part_count):
            bit = part_order(p, bit_count)[bit_count - 1 - step]
            if step == 1:
                locals_[p].wait()
            if pending[p] is not None:
                pending[p].wait_recv()
            index = tuple(
                slice(None) if b in done[p] else mine[b] for b in reversed(range(bit_count))
            )
            view = outs[p].at[index]
            copy = pltpu.make_async_remote_copy(
                src_ref=ins[p] if step == 0 else view,
                dst_ref=view,
                send_sem=send_sem.at[p, step],
                recv_sem=recv_sem.at[p, step],
                device_id=(partner[bit],),
                device_id_type=MESH,
            )
            copy.start()
            pending[p] = copy
            sent.append(copy)
            done[p].append(bit)
    for p in range(part_count):
        pending[p].wait_recv()
    for copy in sent:
        copy.wait_send()


def gather_parts(parts, count):
    bit_count = count.bit_length() - 1
    part_count = len(parts)
    spec = pl.BlockSpec(memory_space=pltpu.VMEM)
    outs = pl.pallas_call(
        functools.partial(gather_kernel, bit_count, part_count),
        out_shape=[
            jax.ShapeDtypeStruct((2,) * bit_count + part.shape, part.dtype) for part in parts
        ],
        in_specs=[spec] * part_count,
        out_specs=[spec] * part_count,
        scratch_shapes=[
            pltpu.SemaphoreType.DMA((part_count, bit_count)),
            pltpu.SemaphoreType.DMA((part_count, bit_count)),
            pltpu.SemaphoreType.DMA((part_count,)),
        ],
        compiler_params=pltpu.CompilerParams(collective_id=0, has_side_effects=True),
        name="gather_parts",
    )(*parts)
    return [out.reshape((count,) + part.shape) for out, part in zip(outs, parts)]


def scatter_kernel(bit_count, part_count, split, vector_count, *refs):
    count = 1 << bit_count
    ins, table_in = refs[:part_count], refs[part_count]
    outs, table_out = refs[part_count + 1 : 2 * part_count + 1], refs[2 * part_count + 1]
    vector_outs = refs[2 * part_count + 2 : 2 * part_count + 2 + vector_count]
    rest = list(refs[2 * part_count + 2 + vector_count :])
    send_sem, recv_sem, table_send, table_recv = rest[:4]
    table_got, table_sum = rest[4:6]
    got = rest[6 : 6 + part_count * bit_count]
    held = rest[6 + part_count * bit_count :]
    mine, partner = place(bit_count)
    greet(partner)
    sent = []

    def table_start(step):
        copy = pltpu.make_async_remote_copy(
            src_ref=table_in if step == 0 else table_sum.at[step - 1],
            dst_ref=table_got.at[step],
            send_sem=table_send.at[step],
            recv_sem=table_recv.at[step],
            device_id=(partner[step],),
            device_id_type=MESH,
        )
        copy.start()
        sent.append(copy)
        return copy

    def start(p, step):
        bit = part_order(p, bit_count)[step]
        source = ins[p] if step == 0 else held[p * (bit_count - 1) + step - 1]
        copy = pltpu.make_async_remote_copy(
            src_ref=source.at[:, 1 - mine[bit]],
            dst_ref=got[p * bit_count + step],
            send_sem=send_sem.at[p, step],
            recv_sem=recv_sem.at[p, step],
            device_id=(partner[bit],),
            device_id_type=MESH,
        )
        copy.start()
        sent.append(copy)
        return copy

    def add(p, step):
        bit = part_order(p, bit_count)[step]
        source = ins[p] if step == 0 else held[p * (bit_count - 1) + step - 1]
        arrived = got[p * bit_count + step]
        high, low = arrived.shape[0], arrived.shape[1]

        def total(k):
            i, j = k // low, k % low
            return source[i, mine[bit], j].astype(jnp.float32) + arrived[i, j].astype(jnp.float32)

        if step == bit_count - 1:
            final = total(0)
            outs[p][...] = final[:, : outs[p].shape[1]]
            if p == part_count - 1:
                for k in range(vector_count):
                    vector_outs[k][...] = final[
                        k : k + 1, split : split + vector_outs[k].shape[1]
                    ]
            return
        target = held[p * (bit_count - 1) + step]
        low_next = target.shape[2]

        def body(k, carry):
            target[k // (2 * low_next), (k // low_next) % 2, k % low_next] = total(k).astype(
                target.dtype
            )
            return carry

        lax.fori_loop(0, high * low, body, 0)

    pending = [start(p, 0) for p in range(part_count)]
    table_pending = table_start(0)
    for step in range(bit_count):
        for p in range(part_count):
            pending[p].wait_recv()
            add(p, step)
            if step + 1 < bit_count:
                pending[p] = start(p, step + 1)
        table_pending.wait_recv()
        total_table = (table_in[...] if step == 0 else table_sum[step - 1]) + table_got[step]
        if step + 1 < bit_count:
            table_sum[step] = total_table
            table_pending = table_start(step + 1)
        else:
            table_out[...] = total_table
    for copy in sent:
        copy.wait_send()


def remaining_shape(order, step):
    left = sorted(order[step:])
    place_of = left.index(order[step])
    return (1 << (len(left) - 1 - place_of), 2, 1 << place_of)


def scatter_parts(parts, table, count, split, lengths):
    bit_count = count.bit_length() - 1
    part_count = len(parts)
    spec = pl.BlockSpec(memory_space=pltpu.VMEM)
    got, held, shaped = [], [], []
    for p, part in enumerate(parts):
        order = part_order(p, bit_count)
        block = part.shape[1:]
        for step in range(bit_count):
            high, two, low = remaining_shape(order, step)
            got.append(pltpu.VMEM((high, low) + block, part.dtype))
            if step == 0:
                shaped.append(part.reshape((high, two, low) + block))
            else:
                held.append(pltpu.VMEM((high, two, low) + block, part.dtype))
    outs = pl.pallas_call(
        functools.partial(scatter_kernel, bit_count, part_count, split, len(lengths)),
        out_shape=[jax.ShapeDtypeStruct(part.shape[1:], jnp.float32) for part in parts[:-1]]
        + [
            jax.ShapeDtypeStruct((parts[-1].shape[1], split), jnp.float32),
            jax.ShapeDtypeStruct(table.shape, jnp.float32),
        ]
        + [jax.ShapeDtypeStruct((1, length), jnp.float32) for length in lengths],
        in_specs=[spec] * (part_count + 1),
        out_specs=[spec] * (part_count + 1 + len(lengths)),
        scratch_shapes=[
            pltpu.SemaphoreType.DMA((part_count, bit_count)),
            pltpu.SemaphoreType.DMA((part_count, bit_count)),
            pltpu.SemaphoreType.DMA((bit_count,)),
            pltpu.SemaphoreType.DMA((bit_count,)),
            pltpu.VMEM((bit_count,) + table.shape, jnp.float32),
            pltpu.VMEM((bit_count,) + table.shape, jnp.float32),
        ]
        + got
        + held,
        compiler_params=pltpu.CompilerParams(collective_id=1, has_side_effects=True),
        name="scatter_parts",
    )(*shaped, table)
    return (outs[:part_count], outs[part_count + 1 :], outs[part_count])


ROWS = 16


def fold(block):
    r, c = block.shape[-2:]
    rows = max(r, ROWS)
    return block.reshape(block.shape[:-2] + (rows, r * c // rows))


def unfold(blocks, r, c):
    return blocks[..., : r * c // blocks.shape[-2]].reshape(blocks.shape[:-2] + (r, c))


def vector_rows(vectors, like):
    rows, width = like.shape[-2:]
    longest = max(v.shape[-1] for v in vectors)
    total = -(-(width + longest) // LANES) * LANES - width
    tile = jnp.zeros(like.shape[:-1] + (total,), like.dtype)
    lead = [(0, 0)] * (like.ndim - 2)
    for k, v in enumerate(vectors):
        tile += jnp.pad(v[..., None, :], lead + [(k, rows - 1 - k), (0, total - v.shape[-1])])
    return tile


def with_vectors(block, vectors):
    return jnp.concatenate([block, vector_rows(vectors, block)], axis=-1)


def fetch_all(shards):
    count = lax.axis_size("fsdp")
    vectors = [shards[k] for k in (0, 1, 3, 5, 6, 7, 9, 11)]
    lengths = [v.shape[0] for v in vectors]
    qkv, proj, fc1, fc2_t = shards[2], shards[4], shards[8], shards[10].T
    folded_proj = fold(proj)
    parts = [
        fold(fc1),
        fold(fc2_t),
        fold(qkv),
        with_vectors(folded_proj, vectors),
    ]
    fc1_all, fc2_all, qkv_all, proj_all = gather_parts(parts, count)

    def whole(blocks, shard):
        r, c = shard.shape
        return unfold(blocks, r, c).reshape(count * r, c)

    at = folded_proj.shape[1]
    gathered = [
        proj_all[:, k, at : at + length].reshape(-1) for k, length in enumerate(lengths)
    ]
    return (
        gathered[0],
        gathered[1],
        whole(qkv_all, qkv),
        gathered[2],
        whole(proj_all, proj),
        gathered[3],
        gathered[4],
        gathered[5],
        whole(fc1_all, fc1),
        gathered[6],
        whole(fc2_all, fc2_t),
        gathered[7],
    )


def scatter_whole(grads, table_local):
    count = lax.axis_size("fsdp")

    def blocks(grad):
        return fold(grad.astype(jnp.bfloat16).reshape(count, grad.shape[0] // count, grad.shape[1]))

    vectors = [
        grads[k].astype(jnp.bfloat16).reshape(count, -1) for k in (0, 1, 3, 5, 6, 7, 9, 11)
    ]
    folded_proj = blocks(grads[4])
    parts = [
        blocks(grads[10]),
        blocks(grads[8]),
        blocks(grads[2]),
        with_vectors(folded_proj, vectors),
    ]
    entries = table_local.size
    table_rows = -(-entries // (8 * LANES)) * 8
    table_pad = jnp.pad(table_local.reshape(-1), (0, table_rows * LANES - entries)).reshape(
        table_rows, LANES
    )
    (fc2_b, fc1_b, qkv_b, proj_b), vector_outs, table_sum = scatter_parts(
        parts, table_pad, count, folded_proj.shape[2], [v.shape[1] for v in vectors]
    )

    def own(block, grad):
        return unfold(block, grad.shape[0] // count, grad.shape[1])

    pieces = [piece[0] for piece in vector_outs]
    table_grad = table_sum.reshape(-1)[:entries].reshape(table_local.shape)
    return (
        (
            pieces[0],
            pieces[1],
            own(qkv_b, grads[2]),
            pieces[2],
            own(proj_b, grads[4]),
            pieces[3],
            pieces[4],
            pieces[5],
            own(fc1_b, grads[8]),
            pieces[6],
            own(fc2_b, grads[10]).T,
            pieces[7],
        ),
        table_grad,
    )


def forward_pass(images, params, lookups):
    (
        gain_one,
        shift_one,
        qkv_weight,
        qv_bias,
        proj_weight,
        proj_bias,
        gain_two,
        shift_two,
        fc1_weight,
        fc1_bias,
        fc2_weight,
        fc2_bias,
    ) = params
    image_count, tok_count, model_width = images.shape
    row_count = image_count * tok_count
    inputs_f = images.astype(jnp.float32).reshape(row_count, model_width)
    normed_one, unit_one, inv_one = normalize(
        inputs_f, gain_one.astype(jnp.float32), shift_one.astype(jnp.float32)
    )
    normed_one = normed_one.astype(jnp.bfloat16)
    qkv_shift = jnp.concatenate(
        [
            qv_bias[:model_width].astype(jnp.float32),
            jnp.zeros((model_width,), jnp.float32),
            qv_bias[model_width:].astype(jnp.float32),
        ]
    )
    qkv_rows = (
        jnp.dot(normed_one, qkv_weight, preferred_element_type=jnp.float32) + qkv_shift
    ).astype(jnp.bfloat16)
    qkv_win, attended = attend(qkv_rows, lookups)
    resid = (
        inputs_f
        + jnp.dot(attended, proj_weight, preferred_element_type=jnp.float32)
        + proj_bias.astype(jnp.float32)
    )
    normed_two, unit_two, inv_two = normalize(
        resid, gain_two.astype(jnp.float32), shift_two.astype(jnp.float32)
    )
    normed_two = normed_two.astype(jnp.bfloat16)
    pre_act = jnp.dot(normed_two, fc1_weight, preferred_element_type=jnp.float32) + fc1_bias.astype(
        jnp.float32
    )
    activ, gelu_slope = gelu_parts(pre_act)
    activ = activ.astype(jnp.bfloat16)
    output = (
        resid
        + jnp.dot(activ, fc2_weight.T, preferred_element_type=jnp.float32)
        + fc2_bias.astype(jnp.float32)
    ).astype(jnp.bfloat16)
    saved = (
        unit_one,
        inv_one,
        normed_one,
        qkv_win,
        attended,
        unit_two,
        inv_two,
        normed_two,
        gelu_slope,
        activ,
    )
    return (output.reshape(image_count, tok_count, model_width), saved)


def backward_pass(cotangent, saved, params, lookups):
    (
        gain_one,
        shift_one,
        qkv_weight,
        qv_bias,
        proj_weight,
        proj_bias,
        gain_two,
        shift_two,
        fc1_weight,
        fc1_bias,
        fc2_weight,
        fc2_bias,
    ) = params
    (
        unit_one,
        inv_one,
        normed_one,
        qkv_win,
        attended,
        unit_two,
        inv_two,
        normed_two,
        gelu_slope,
        activ,
    ) = saved
    image_count, tok_count, model_width = cotangent.shape
    row_count = image_count * tok_count
    cot_rows = cotangent.reshape(row_count, model_width)
    cot_f = cot_rows.astype(jnp.float32)
    fc2_grad = jnp.dot(cot_rows.T, activ, preferred_element_type=jnp.float32)
    fc2_bias_grad = jnp.sum(cot_f, axis=0)
    grad_pre = jnp.dot(cot_rows, fc2_weight, preferred_element_type=jnp.float32) * gelu_slope
    grad_pre_b = grad_pre.astype(jnp.bfloat16)
    fc1_grad = jnp.dot(normed_two.T, grad_pre_b, preferred_element_type=jnp.float32)
    fc1_bias_grad = jnp.sum(grad_pre, axis=0)
    grad_normed = jnp.dot(grad_pre_b, fc1_weight.T, preferred_element_type=jnp.float32)
    grad_mid, gain_two_grad, shift_two_grad = norm_backward(
        grad_normed, unit_two, inv_two, gain_two.astype(jnp.float32)
    )
    grad_resid = cot_f + grad_mid
    grad_resid_b = grad_resid.astype(jnp.bfloat16)
    proj_grad = jnp.dot(attended.T, grad_resid_b, preferred_element_type=jnp.float32)
    proj_bias_grad = jnp.sum(grad_resid, axis=0)
    grad_att = jnp.dot(grad_resid_b, proj_weight.T, preferred_element_type=jnp.float32).astype(
        jnp.bfloat16
    )
    qkv_grad_b, column_sums, pair_grad = attend_back(qkv_win, grad_att, lookups)
    column_sums = column_sums[0]
    qkv_grad_w = jnp.dot(normed_one.T, qkv_grad_b, preferred_element_type=jnp.float32)
    qv_grad = jnp.concatenate([column_sums[:model_width], column_sums[2 * model_width :]])
    grad_first = jnp.dot(qkv_grad_b, qkv_weight.T, preferred_element_type=jnp.float32)
    grad_low, gain_one_grad, shift_one_grad = norm_backward(
        grad_first, unit_one, inv_one, gain_one.astype(jnp.float32)
    )
    input_grad = (grad_resid + grad_low).reshape(image_count, tok_count, model_width)
    grads = (
        gain_one_grad,
        shift_one_grad,
        qkv_grad_w,
        qv_grad,
        proj_grad,
        proj_bias_grad,
        gain_two_grad,
        shift_two_grad,
        fc1_grad,
        fc1_bias_grad,
        fc2_grad,
        fc2_bias_grad,
    )
    return (input_grad, grads, pair_grad)


def per_device(
    block_input,
    out_cotangent,
    norm1_gain,
    norm1_bias,
    qkv_weight,
    qv_bias,
    proj_weight,
    proj_bias,
    norm2_gain,
    norm2_bias,
    fc1_weight,
    fc1_bias,
    fc2_weight,
    fc2_bias,
    bias_table,
    window_mask,
    rel_index,
    partition,
):
    shards = (
        norm1_gain,
        norm1_bias,
        qkv_weight,
        qv_bias,
        proj_weight,
        proj_bias,
        norm2_gain,
        norm2_bias,
        fc1_weight,
        fc1_bias,
        fc2_weight,
        fc2_bias,
    )
    pair_count = WINDOW * WINDOW
    table_rows = bias_table.shape[0]
    one_hot = (
        rel_index.reshape(pair_count, 1) == jnp.arange(table_rows, dtype=jnp.int32)[None, :]
    ).astype(jnp.float32)
    table_bias = jnp.transpose(
        jnp.dot(one_hot, bias_table.astype(jnp.float32), precision=lax.Precision.HIGHEST).reshape(
            WINDOW, WINDOW, HEADS
        ),
        (2, 0, 1),
    )
    lookups = attention_tables(table_bias, window_mask, partition)
    held_params = fetch_all(shards)
    micro_index = 0
    output, saved = forward_pass(block_input, held_params, lookups)
    kept = [saved]
    input_grads = [None] * MICRO
    pair_total = jnp.zeros((HEADS, WINDOW, WINDOW), jnp.float32)
    grad_totals = None
    for micro_index in reversed(range(MICRO)):
        input_grad, grads, pair_grad = backward_pass(
            out_cotangent, kept[micro_index], held_params, lookups
        )
        input_grads[micro_index] = input_grad
        pair_total = pair_grad
        grad_totals = grads
    table_local = jnp.dot(
        one_hot.T,
        jnp.transpose(pair_total, (1, 2, 0)).reshape(pair_count, HEADS),
        precision=lax.Precision.HIGHEST,
    )
    grad_totals, table_grad = scatter_whole(grad_totals, table_local)
    input_grad_all = input_grads[0]
    return (
        output,
        input_grad_all,
        grad_totals[0],
        grad_totals[1],
        grad_totals[2],
        grad_totals[3],
        grad_totals[4],
        grad_totals[5],
        grad_totals[6],
        grad_totals[7],
        grad_totals[8],
        grad_totals[9],
        grad_totals[10],
        grad_totals[11],
        table_grad,
    )


def solution(mesh):
    placed = (
        P("fsdp", None, None),
        P("fsdp", None, None),
        P("fsdp"),
        P("fsdp"),
        P("fsdp", None),
        P("fsdp"),
        P("fsdp", None),
        P("fsdp"),
        P("fsdp"),
        P("fsdp"),
        P("fsdp", None),
        P("fsdp"),
        P(None, "fsdp"),
        P("fsdp"),
        P(),
        P(),
        P(),
        P(),
    )
    return jax.shard_map(
        per_device,
        mesh=mesh,
        in_specs=placed,
        out_specs=(
            P("fsdp", None, None),
            P("fsdp", None, None),
            P("fsdp"),
            P("fsdp"),
            P("fsdp", None),
            P("fsdp"),
            P("fsdp", None),
            P("fsdp"),
            P("fsdp"),
            P("fsdp"),
            P("fsdp", None),
            P("fsdp"),
            P(None, "fsdp"),
            P("fsdp"),
            P(),
        ),
        check_vma=False,
    )
```

```python
import functools

import jax
import jax.numpy as jnp
from jax import lax
from jax.experimental import pallas as pl
from jax.experimental.pallas import tpu as pltpu
from jax.sharding import PartitionSpec as P

HEADS = 16
WINDOW = 49
WIN_IMG = 4
MICRO = 1


EPSILON = 1e-05
NEG_FILL = -1e30
ROOT_HALF = 0.7071067811865476
DENSITY = 0.3989422804014327


def normalize(values, gain_vec, shift_vec):
    center = values - jnp.mean(values, axis=-1, keepdims=True)
    inv_std = lax.rsqrt(jnp.mean(center * center, axis=-1, keepdims=True) + EPSILON)
    unit_rows = center * inv_std
    return (unit_rows * gain_vec + shift_vec, unit_rows, inv_std)


def norm_backward(grad_out, unit_rows, inv_std, gain_vec):
    scaled = grad_out * gain_vec
    grad_in = inv_std * (
        scaled
        - jnp.mean(scaled, axis=-1, keepdims=True)
        - unit_rows * jnp.mean(scaled * unit_rows, axis=-1, keepdims=True)
    )
    return (grad_in, jnp.sum(grad_out * unit_rows, axis=0), jnp.sum(grad_out, axis=0))


def gelu_parts(pre_act):
    normal_cdf = 0.5 * (1.0 + jax.scipy.special.erf(pre_act * ROOT_HALF))
    normal_pdf = jnp.exp(-0.5 * pre_act * pre_act) * DENSITY
    return (pre_act * normal_cdf, normal_cdf + pre_act * normal_pdf)


NT = (((1,), (1,)), ((), ()))
TN = (((0,), (0,)), ((), ()))


def mul(left, right, dims=(((1,), (0,)), ((), ()))):
    return lax.dot_general(left, right, dims, preferred_element_type=jnp.float32)


def pair_mask(mask_ref, spread, same_ref):
    return (mul(mask_ref[...], spread) > 0.5) & (same_ref[...] > 0)


def head_scores(query, key_block, bias, spread_t, spread, allowed, scale):
    wide = mul(mul(spread_t, bias).astype(jnp.bfloat16), spread)
    return jnp.where(allowed, mul(query, key_block, NT) * scale + wide, NEG_FILL)


def soft_rows(scores):
    row_top = jnp.max(scores, axis=-1, keepdims=True)
    log_total = row_top + jnp.log(jnp.sum(jnp.exp(scores - row_top), axis=-1, keepdims=True))
    return jnp.exp(scores - log_total)


def head_lanes(rows, lanes, width, h):
    lane = lax.broadcasted_iota(jnp.int32, (rows, lanes), 1)
    return (lane >= h * width) & (lane < (h + 1) * width)


def attend_kernel(
    width, qkv_ref, pick_ref, back_ref, bias_ref, mask_ref, same_ref, spread_ref, spread_t_ref,
    qkv_win_ref, out_ref
):
    rows, model = out_ref.shape
    spread, spread_t = spread_ref[...], spread_t_ref[...]
    allowed = pair_mask(mask_ref, spread, same_ref)
    qkv_win_ref[...] = mul(pick_ref[...], qkv_ref[...]).astype(jnp.bfloat16)
    heads = LANES // width
    for group in range(model // LANES):
        low = group * LANES
        query = qkv_win_ref[:, low : low + LANES]
        keys = qkv_win_ref[:, model + low : model + low + LANES]
        values = qkv_win_ref[:, 2 * model + low : 2 * model + low + LANES]
        total = jnp.zeros((rows, LANES), jnp.float32)
        for h in range(heads):
            lanes = head_lanes(rows, LANES, width, h)
            scores = head_scores(
                jnp.where(lanes, query, jnp.zeros_like(query)),
                keys,
                bias_ref[group * heads + h],
                spread_t,
                spread,
                allowed,
                width ** (-0.5),
            )
            probs = soft_rows(scores).astype(jnp.bfloat16)
            total = jnp.where(lanes, mul(probs, values), total)
        out_ref[:, low : low + LANES] = mul(back_ref[...], total.astype(jnp.bfloat16)).astype(
            jnp.bfloat16
        )


def attend_back_kernel(
    width, qkv_win_ref, grad_ref, pick_ref, back_ref, bias_ref, mask_ref, same_ref, spread_ref,
    spread_t_ref, out_ref, sums_ref, pair_ref
):
    rows, model = grad_ref.shape
    spread, spread_t = spread_ref[...], spread_t_ref[...]
    allowed = pair_mask(mask_ref, spread, same_ref)
    heads = LANES // width
    scale = width ** (-0.5)
    for group in range(model // LANES):
        low = group * LANES
        query = qkv_win_ref[:, low : low + LANES]
        keys = qkv_win_ref[:, model + low : model + low + LANES]
        values = qkv_win_ref[:, 2 * model + low : 2 * model + low + LANES]
        grad = mul(pick_ref[...], grad_ref[:, low : low + LANES]).astype(jnp.bfloat16)
        totals = [jnp.zeros((rows, LANES), jnp.float32) for _ in range(3)]
        for h in range(heads):
            lanes = head_lanes(rows, LANES, width, h)
            scores = head_scores(
                jnp.where(lanes, query, jnp.zeros_like(query)),
                keys,
                bias_ref[group * heads + h],
                spread_t,
                spread,
                allowed,
                scale,
            )
            soft = soft_rows(scores)
            prob_grad = mul(jnp.where(lanes, grad, jnp.zeros_like(grad)), values, NT)
            inner = jnp.sum(soft * prob_grad, axis=-1, keepdims=True)
            score_grad = soft * (prob_grad - inner)
            coarse = score_grad.astype(jnp.bfloat16)
            fine = (score_grad - coarse.astype(jnp.float32)).astype(jnp.bfloat16)
            pair = jnp.zeros(pair_ref.shape[1:], jnp.float32)
            for piece in (coarse, fine):
                pair += mul(mul(spread, piece).astype(jnp.bfloat16), spread_t)
            pair_ref[group * heads + h] = pair
            totals[0] = jnp.where(lanes, mul(coarse, keys) * scale, totals[0])
            totals[1] = jnp.where(lanes, mul(coarse, query, TN) * scale, totals[1])
            totals[2] = jnp.where(lanes, mul(soft.astype(jnp.bfloat16), grad, TN), totals[2])
        for k in range(3):
            at = k * model + low
            sums_ref[:, at : at + LANES] = jnp.sum(totals[k], axis=0, keepdims=True)
            out_ref[:, at : at + LANES] = mul(
                back_ref[...], totals[k].astype(jnp.bfloat16)
            ).astype(jnp.bfloat16)


def attention_tables(bias_heads, window_mask, partition):
    tokens = partition.shape[0]
    span = window_mask.shape[-1]
    token = jnp.arange(tokens, dtype=jnp.int32)
    pick = (partition[:, None] == token[None, :]).astype(jnp.bfloat16)
    back = (partition[None, :] == token[:, None]).astype(jnp.bfloat16)
    same = (token[:, None] // span == token[None, :] // span).astype(jnp.float32)
    spread = (token[None, :] % span == jnp.arange(span)[:, None]).astype(jnp.bfloat16)
    mask_rows = (window_mask == 1).astype(jnp.bfloat16).reshape(tokens, span)
    return (pick, back, bias_heads.astype(jnp.bfloat16), mask_rows, same, spread, spread.T)


def attend(qkv_rows, tables):
    rows, wide = qkv_rows.shape
    model = wide // 3
    spec = pl.BlockSpec(memory_space=pltpu.VMEM)
    return pl.pallas_call(
        functools.partial(attend_kernel, model // HEADS),
        out_shape=[
            jax.ShapeDtypeStruct((rows, wide), jnp.bfloat16),
            jax.ShapeDtypeStruct((rows, model), jnp.bfloat16),
        ],
        in_specs=[spec] * 8,
        out_specs=[spec] * 2,
        name="attend",
    )(qkv_rows, *tables)


def attend_back(qkv_win, grad_att, tables):
    rows, wide = qkv_win.shape
    model = wide // 3
    span = tables[3].shape[1]
    spec = pl.BlockSpec(memory_space=pltpu.VMEM)
    return pl.pallas_call(
        functools.partial(attend_back_kernel, model // HEADS),
        out_shape=[
            jax.ShapeDtypeStruct((rows, wide), jnp.bfloat16),
            jax.ShapeDtypeStruct((1, wide), jnp.float32),
            jax.ShapeDtypeStruct((HEADS, span, span), jnp.float32),
        ],
        in_specs=[spec] * 9,
        out_specs=[spec] * 3,
        name="attend_back",
    )(qkv_win, grad_att, *tables)


LANES = 128
MESH = pl.DeviceIdType.MESH


def bit_orders(bit_count):
    rest = list(range(1, bit_count))
    return ([0] + rest, [0] + rest[1:] + rest[:1])


def part_order(part, bit_count):
    return bit_orders(bit_count)[part % 2]


def place(bit_count):
    me = lax.axis_index("fsdp")
    mine = [lax.rem(lax.div(me, 1 << b), 2) for b in range(bit_count)]
    partner = [me + (1 - 2 * mine[b]) * (1 << b) for b in range(bit_count)]
    return (mine, partner)


def greet(partner):
    barrier = pltpu.get_barrier_semaphore()
    for other in partner:
        pl.semaphore_signal(barrier, inc=1, device_id=(other,), device_id_type=MESH)
    pl.semaphore_wait(barrier, len(partner))


def gather_kernel(bit_count, part_count, *refs):
    ins, outs = refs[:part_count], refs[part_count : 2 * part_count]
    send_sem, recv_sem, local_sem = refs[2 * part_count :]
    mine, partner = place(bit_count)
    locals_ = []
    whole_index = tuple(mine[b] for b in reversed(range(bit_count)))
    for p in range(part_count):
        copy = pltpu.make_async_copy(ins[p], outs[p].at[whole_index], local_sem.at[p])
        copy.start()
        locals_.append(copy)
    greet(partner)
    pending = [None] * part_count
    sent = []
    done = [[] for _ in range(part_count)]
    for step in range(bit_count):
        for p in range(part_count):
            bit = part_order(p, bit_count)[bit_count - 1 - step]
            if step == 1:
                locals_[p].wait()
            if pending[p] is not None:
                pending[p].wait_recv()
            index = tuple(
                slice(None) if b in done[p] else mine[b] for b in reversed(range(bit_count))
            )
            view = outs[p].at[index]
            copy = pltpu.make_async_remote_copy(
                src_ref=ins[p] if step == 0 else view,
                dst_ref=view,
                send_sem=send_sem.at[p, step],
                recv_sem=recv_sem.at[p, step],
                device_id=(partner[bit],),
                device_id_type=MESH,
            )
            copy.start()
            pending[p] = copy
            sent.append(copy)
            done[p].append(bit)
    for p in range(part_count):
        pending[p].wait_recv()
    for copy in sent:
        copy.wait_send()


def gather_parts(parts, count):
    bit_count = count.bit_length() - 1
    part_count = len(parts)
    spec = pl.BlockSpec(memory_space=pltpu.VMEM)
    outs = pl.pallas_call(
        functools.partial(gather_kernel, bit_count, part_count),
        out_shape=[
            jax.ShapeDtypeStruct((2,) * bit_count + part.shape, part.dtype) for part in parts
        ],
        in_specs=[spec] * part_count,
        out_specs=[spec] * part_count,
        scratch_shapes=[
            pltpu.SemaphoreType.DMA((part_count, bit_count)),
            pltpu.SemaphoreType.DMA((part_count, bit_count)),
            pltpu.SemaphoreType.DMA((part_count,)),
        ],
        compiler_params=pltpu.CompilerParams(collective_id=0, has_side_effects=True),
        name="gather_parts",
    )(*parts)
    return [out.reshape((count,) + part.shape) for out, part in zip(outs, parts)]


def scatter_kernel(bit_count, part_count, split, vector_count, *refs):
    count = 1 << bit_count
    ins, table_in = refs[:part_count], refs[part_count]
    outs, table_out = refs[part_count + 1 : 2 * part_count + 1], refs[2 * part_count + 1]
    vector_outs = refs[2 * part_count + 2 : 2 * part_count + 2 + vector_count]
    rest = list(refs[2 * part_count + 2 + vector_count :])
    send_sem, recv_sem, table_send, table_recv = rest[:4]
    table_got, table_sum = rest[4:6]
    got = rest[6 : 6 + part_count * bit_count]
    held = rest[6 + part_count * bit_count :]
    mine, partner = place(bit_count)
    greet(partner)
    sent = []

    def table_start(step):
        copy = pltpu.make_async_remote_copy(
            src_ref=table_in if step == 0 else table_sum.at[step - 1],
            dst_ref=table_got.at[step],
            send_sem=table_send.at[step],
            recv_sem=table_recv.at[step],
            device_id=(partner[step],),
            device_id_type=MESH,
        )
        copy.start()
        sent.append(copy)
        return copy

    def start(p, step):
        bit = part_order(p, bit_count)[step]
        source = ins[p] if step == 0 else held[p * (bit_count - 1) + step - 1]
        copy = pltpu.make_async_remote_copy(
            src_ref=source.at[:, 1 - mine[bit]],
            dst_ref=got[p * bit_count + step],
            send_sem=send_sem.at[p, step],
            recv_sem=recv_sem.at[p, step],
            device_id=(partner[bit],),
            device_id_type=MESH,
        )
        copy.start()
        sent.append(copy)
        return copy

    def add(p, step):
        bit = part_order(p, bit_count)[step]
        source = ins[p] if step == 0 else held[p * (bit_count - 1) + step - 1]
        arrived = got[p * bit_count + step]
        high, low = arrived.shape[0], arrived.shape[1]

        def total(k):
            i, j = k // low, k % low
            return source[i, mine[bit], j].astype(jnp.float32) + arrived[i, j].astype(jnp.float32)

        if step == bit_count - 1:
            final = total(0)
            outs[p][...] = final[:, : outs[p].shape[1]]
            if p == part_count - 1:
                for k in range(vector_count):
                    vector_outs[k][...] = final[
                        k : k + 1, split : split + vector_outs[k].shape[1]
                    ]
            return
        target = held[p * (bit_count - 1) + step]
        low_next = target.shape[2]

        def body(k, carry):
            target[k // (2 * low_next), (k // low_next) % 2, k % low_next] = total(k).astype(
                target.dtype
            )
            return carry

        lax.fori_loop(0, high * low, body, 0)

    pending = [start(p, 0) for p in range(part_count)]
    table_pending = table_start(0)
    for step in range(bit_count):
        for p in range(part_count):
            pending[p].wait_recv()
            add(p, step)
            if step + 1 < bit_count:
                pending[p] = start(p, step + 1)
        table_pending.wait_recv()
        total_table = (table_in[...] if step == 0 else table_sum[step - 1]) + table_got[step]
        if step + 1 < bit_count:
            table_sum[step] = total_table
            table_pending = table_start(step + 1)
        else:
            table_out[...] = total_table
    for copy in sent:
        copy.wait_send()


def remaining_shape(order, step):
    left = sorted(order[step:])
    place_of = left.index(order[step])
    return (1 << (len(left) - 1 - place_of), 2, 1 << place_of)


def settle_kernel(*refs):
    half = len(refs) // 2
    for source, target in zip(refs[:half], refs[half:]):
        target[...] = source[...]


def settle(arrays):
    spec = pl.BlockSpec(memory_space=pltpu.VMEM)
    return list(
        pl.pallas_call(
            settle_kernel,
            out_shape=[jax.ShapeDtypeStruct(a.shape, a.dtype) for a in arrays],
            in_specs=[spec] * len(arrays),
            out_specs=[spec] * len(arrays),
            name="settle",
        )(*arrays)
    )


def scatter_parts(parts, table, count, split, lengths):
    bit_count = count.bit_length() - 1
    part_count = len(parts)
    spec = pl.BlockSpec(memory_space=pltpu.VMEM)
    got, held, shaped = [], [], []
    for p, part in enumerate(parts):
        order = part_order(p, bit_count)
        block = part.shape[1:]
        for step in range(bit_count):
            high, two, low = remaining_shape(order, step)
            got.append(pltpu.VMEM((high, low) + block, part.dtype))
            if step == 0:
                shaped.append(part.reshape((high, two, low) + block))
            else:
                held.append(pltpu.VMEM((high, two, low) + block, part.dtype))
    outs = pl.pallas_call(
        functools.partial(scatter_kernel, bit_count, part_count, split, len(lengths)),
        out_shape=[jax.ShapeDtypeStruct(part.shape[1:], jnp.float32) for part in parts[:-1]]
        + [
            jax.ShapeDtypeStruct((parts[-1].shape[1], split), jnp.float32),
            jax.ShapeDtypeStruct(table.shape, jnp.float32),
        ]
        + [jax.ShapeDtypeStruct((1, length), jnp.float32) for length in lengths],
        in_specs=[spec] * (part_count + 1),
        out_specs=[spec] * (part_count + 1 + len(lengths)),
        scratch_shapes=[
            pltpu.SemaphoreType.DMA((part_count, bit_count)),
            pltpu.SemaphoreType.DMA((part_count, bit_count)),
            pltpu.SemaphoreType.DMA((bit_count,)),
            pltpu.SemaphoreType.DMA((bit_count,)),
            pltpu.VMEM((bit_count,) + table.shape, jnp.float32),
            pltpu.VMEM((bit_count,) + table.shape, jnp.float32),
        ]
        + got
        + held,
        compiler_params=pltpu.CompilerParams(collective_id=1, has_side_effects=True),
        name="scatter_parts",
    )(*shaped, table)
    outs = settle(outs)
    return (outs[:part_count], outs[part_count + 1 :], outs[part_count])


ROWS = 16


def fold(block):
    r, c = block.shape[-2:]
    rows = max(r, ROWS)
    return block.reshape(block.shape[:-2] + (rows, r * c // rows))


def unfold(blocks, r, c):
    return blocks[..., : r * c // blocks.shape[-2]].reshape(blocks.shape[:-2] + (r, c))


def vector_rows(vectors, like):
    rows, width = like.shape[-2:]
    longest = max(v.shape[-1] for v in vectors)
    total = -(-(width + longest) // LANES) * LANES - width
    tile = jnp.zeros(like.shape[:-1] + (total,), like.dtype)
    lead = [(0, 0)] * (like.ndim - 2)
    for k, v in enumerate(vectors):
        tile += jnp.pad(v[..., None, :], lead + [(k, rows - 1 - k), (0, total - v.shape[-1])])
    return tile


def with_vectors(block, vectors):
    return jnp.concatenate([block, vector_rows(vectors, block)], axis=-1)


def fetch_all(shards):
    count = lax.axis_size("fsdp")
    vectors = [shards[k] for k in (0, 1, 3, 5, 6, 7, 9, 11)]
    lengths = [v.shape[0] for v in vectors]
    qkv, proj, fc1, fc2_t = shards[2], shards[4], shards[8], shards[10].T
    folded_proj = fold(proj)
    parts = [
        fold(fc1),
        fold(fc2_t),
        fold(qkv),
        with_vectors(folded_proj, vectors),
    ]
    fc1_all, fc2_all, qkv_all, proj_all = gather_parts(parts, count)

    def whole(blocks, shard):
        r, c = shard.shape
        return unfold(blocks, r, c).reshape(count * r, c)

    at = folded_proj.shape[1]
    gathered = [
        proj_all[:, k, at : at + length].reshape(-1) for k, length in enumerate(lengths)
    ]
    return (
        gathered[0],
        gathered[1],
        whole(qkv_all, qkv),
        gathered[2],
        whole(proj_all, proj),
        gathered[3],
        gathered[4],
        gathered[5],
        whole(fc1_all, fc1),
        gathered[6],
        whole(fc2_all, fc2_t),
        gathered[7],
    )


def scatter_whole(grads, table_local):
    count = lax.axis_size("fsdp")

    def blocks(grad):
        return fold(grad.astype(jnp.bfloat16).reshape(count, grad.shape[0] // count, grad.shape[1]))

    vectors = [
        grads[k].astype(jnp.bfloat16).reshape(count, -1) for k in (0, 1, 3, 5, 6, 7, 9, 11)
    ]
    folded_proj = blocks(grads[4])
    parts = [
        blocks(grads[10]),
        blocks(grads[8]),
        blocks(grads[2]),
        with_vectors(folded_proj, vectors),
    ]
    entries = table_local.size
    table_rows = -(-entries // (8 * LANES)) * 8
    table_pad = jnp.pad(table_local.reshape(-1), (0, table_rows * LANES - entries)).reshape(
        table_rows, LANES
    )
    (fc2_b, fc1_b, qkv_b, proj_b), vector_outs, table_sum = scatter_parts(
        parts, table_pad, count, folded_proj.shape[2], [v.shape[1] for v in vectors]
    )

    def own(block, grad):
        return unfold(block, grad.shape[0] // count, grad.shape[1])

    pieces = [piece[0] for piece in vector_outs]
    table_grad = table_sum.reshape(-1)[:entries].reshape(table_local.shape)
    return (
        (
            pieces[0],
            pieces[1],
            own(qkv_b, grads[2]),
            pieces[2],
            own(proj_b, grads[4]),
            pieces[3],
            pieces[4],
            pieces[5],
            own(fc1_b, grads[8]),
            pieces[6],
            own(fc2_b, grads[10]).T,
            pieces[7],
        ),
        table_grad,
    )


def forward_pass(images, params, lookups):
    (
        gain_one,
        shift_one,
        qkv_weight,
        qv_bias,
        proj_weight,
        proj_bias,
        gain_two,
        shift_two,
        fc1_weight,
        fc1_bias,
        fc2_weight,
        fc2_bias,
    ) = params
    image_count, tok_count, model_width = images.shape
    row_count = image_count * tok_count
    inputs_f = images.astype(jnp.float32).reshape(row_count, model_width)
    normed_one, unit_one, inv_one = normalize(
        inputs_f, gain_one.astype(jnp.float32), shift_one.astype(jnp.float32)
    )
    normed_one = normed_one.astype(jnp.bfloat16)
    qkv_shift = jnp.concatenate(
        [
            qv_bias[:model_width].astype(jnp.float32),
            jnp.zeros((model_width,), jnp.float32),
            qv_bias[model_width:].astype(jnp.float32),
        ]
    )
    qkv_rows = (
        jnp.dot(normed_one, qkv_weight, preferred_element_type=jnp.float32) + qkv_shift
    ).astype(jnp.bfloat16)
    qkv_win, attended = attend(qkv_rows, lookups)
    resid = (
        inputs_f
        + jnp.dot(attended, proj_weight, preferred_element_type=jnp.float32)
        + proj_bias.astype(jnp.float32)
    )
    normed_two, unit_two, inv_two = normalize(
        resid, gain_two.astype(jnp.float32), shift_two.astype(jnp.float32)
    )
    normed_two = normed_two.astype(jnp.bfloat16)
    pre_act = jnp.dot(normed_two, fc1_weight, preferred_element_type=jnp.float32) + fc1_bias.astype(
        jnp.float32
    )
    activ, gelu_slope = gelu_parts(pre_act)
    activ = activ.astype(jnp.bfloat16)
    output = (
        resid
        + jnp.dot(activ, fc2_weight.T, preferred_element_type=jnp.float32)
        + fc2_bias.astype(jnp.float32)
    ).astype(jnp.bfloat16)
    saved = (
        unit_one,
        inv_one,
        normed_one,
        qkv_win,
        attended,
        unit_two,
        inv_two,
        normed_two,
        gelu_slope,
        activ,
    )
    return (output.reshape(image_count, tok_count, model_width), saved)


def backward_pass(cotangent, saved, params, lookups):
    (
        gain_one,
        shift_one,
        qkv_weight,
        qv_bias,
        proj_weight,
        proj_bias,
        gain_two,
        shift_two,
        fc1_weight,
        fc1_bias,
        fc2_weight,
        fc2_bias,
    ) = params
    (
        unit_one,
        inv_one,
        normed_one,
        qkv_win,
        attended,
        unit_two,
        inv_two,
        normed_two,
        gelu_slope,
        activ,
    ) = saved
    image_count, tok_count, model_width = cotangent.shape
    row_count = image_count * tok_count
    cot_rows = cotangent.reshape(row_count, model_width)
    cot_f = cot_rows.astype(jnp.float32)
    fc2_grad = jnp.dot(cot_rows.T, activ, preferred_element_type=jnp.float32)
    fc2_bias_grad = jnp.sum(cot_f, axis=0)
    grad_pre = jnp.dot(cot_rows, fc2_weight, preferred_element_type=jnp.float32) * gelu_slope
    grad_pre_b = grad_pre.astype(jnp.bfloat16)
    fc1_grad = jnp.dot(normed_two.T, grad_pre_b, preferred_element_type=jnp.float32)
    fc1_bias_grad = jnp.sum(grad_pre, axis=0)
    grad_normed = jnp.dot(grad_pre_b, fc1_weight.T, preferred_element_type=jnp.float32)
    grad_mid, gain_two_grad, shift_two_grad = norm_backward(
        grad_normed, unit_two, inv_two, gain_two.astype(jnp.float32)
    )
    grad_resid = cot_f + grad_mid
    grad_resid_b = grad_resid.astype(jnp.bfloat16)
    proj_grad = jnp.dot(attended.T, grad_resid_b, preferred_element_type=jnp.float32)
    proj_bias_grad = jnp.sum(grad_resid, axis=0)
    grad_att = jnp.dot(grad_resid_b, proj_weight.T, preferred_element_type=jnp.float32).astype(
        jnp.bfloat16
    )
    qkv_grad_b, column_sums, pair_grad = attend_back(qkv_win, grad_att, lookups)
    column_sums = column_sums[0]
    qkv_grad_w = jnp.dot(normed_one.T, qkv_grad_b, preferred_element_type=jnp.float32)
    qv_grad = jnp.concatenate([column_sums[:model_width], column_sums[2 * model_width :]])
    grad_first = jnp.dot(qkv_grad_b, qkv_weight.T, preferred_element_type=jnp.float32)
    grad_low, gain_one_grad, shift_one_grad = norm_backward(
        grad_first, unit_one, inv_one, gain_one.astype(jnp.float32)
    )
    input_grad = (grad_resid + grad_low).reshape(image_count, tok_count, model_width)
    grads = (
        gain_one_grad,
        shift_one_grad,
        qkv_grad_w,
        qv_grad,
        proj_grad,
        proj_bias_grad,
        gain_two_grad,
        shift_two_grad,
        fc1_grad,
        fc1_bias_grad,
        fc2_grad,
        fc2_bias_grad,
    )
    return (input_grad, grads, pair_grad)


def per_device(
    block_input,
    out_cotangent,
    norm1_gain,
    norm1_bias,
    qkv_weight,
    qv_bias,
    proj_weight,
    proj_bias,
    norm2_gain,
    norm2_bias,
    fc1_weight,
    fc1_bias,
    fc2_weight,
    fc2_bias,
    bias_table,
    window_mask,
    rel_index,
    partition,
):
    shards = (
        norm1_gain,
        norm1_bias,
        qkv_weight,
        qv_bias,
        proj_weight,
        proj_bias,
        norm2_gain,
        norm2_bias,
        fc1_weight,
        fc1_bias,
        fc2_weight,
        fc2_bias,
    )
    pair_count = WINDOW * WINDOW
    table_rows = bias_table.shape[0]
    one_hot = (
        rel_index.reshape(pair_count, 1) == jnp.arange(table_rows, dtype=jnp.int32)[None, :]
    ).astype(jnp.float32)
    table_bias = jnp.transpose(
        jnp.dot(one_hot, bias_table.astype(jnp.float32), precision=lax.Precision.HIGHEST).reshape(
            WINDOW, WINDOW, HEADS
        ),
        (2, 0, 1),
    )
    lookups = attention_tables(table_bias, window_mask, partition)
    held_params = fetch_all(shards)
    micro_index = 0
    output, saved = forward_pass(block_input, held_params, lookups)
    kept = [saved]
    input_grads = [None] * MICRO
    pair_total = jnp.zeros((HEADS, WINDOW, WINDOW), jnp.float32)
    grad_totals = None
    for micro_index in reversed(range(MICRO)):
        input_grad, grads, pair_grad = backward_pass(
            out_cotangent, kept[micro_index], held_params, lookups
        )
        input_grads[micro_index] = input_grad
        pair_total = pair_grad
        grad_totals = grads
    table_local = jnp.dot(
        one_hot.T,
        jnp.transpose(pair_total, (1, 2, 0)).reshape(pair_count, HEADS),
        precision=lax.Precision.HIGHEST,
    )
    grad_totals, table_grad = scatter_whole(grad_totals, table_local)
    input_grad_all = input_grads[0]
    return (
        output,
        input_grad_all,
        grad_totals[0],
        grad_totals[1],
        grad_totals[2],
        grad_totals[3],
        grad_totals[4],
        grad_totals[5],
        grad_totals[6],
        grad_totals[7],
        grad_totals[8],
        grad_totals[9],
        grad_totals[10],
        grad_totals[11],
        table_grad,
    )


def solution(mesh):
    placed = (
        P("fsdp", None, None),
        P("fsdp", None, None),
        P("fsdp"),
        P("fsdp"),
        P("fsdp", None),
        P("fsdp"),
        P("fsdp", None),
        P("fsdp"),
        P("fsdp"),
        P("fsdp"),
        P("fsdp", None),
        P("fsdp"),
        P(None, "fsdp"),
        P("fsdp"),
        P(),
        P(),
        P(),
        P(),
    )
    return jax.shard_map(
        per_device,
        mesh=mesh,
        in_specs=placed,
        out_specs=(
            P("fsdp", None, None),
            P("fsdp", None, None),
            P("fsdp"),
            P("fsdp"),
            P("fsdp", None),
            P("fsdp"),
            P("fsdp", None),
            P("fsdp"),
            P("fsdp"),
            P("fsdp"),
            P("fsdp", None),
            P("fsdp"),
            P(None, "fsdp"),
            P("fsdp"),
            P(),
        ),
        check_vma=False,
    )
```
